128 devices in a mesh: seq: 16 (over x_lo, z, core), tp: 8 (over y, x_hi).
Axes of the slice: x: 4 (x_hi: 2, x_lo: 2; x = x_hi * 2 + x_lo), y: 4, z: 4, core: 2. Of those that a mesh axis runs over, the one named last changes fastest.
Arguments:
- hidden_in: bfloat16 [6144, 3584], P('seq'), may hold values from -48 to 48
- joined_inputs: bfloat16 [6144, 8192], P('seq', 'tp'), may hold values from -64 to 64
- lengths: int32 [4], replicated, may hold values from 1 to 3072, 6144 in all
- o_weight: bfloat16 [4096, 3584], P('tp'), may hold values from -0.09375 to 0.09375
- gate_up: float32 [2, 3584, 7168], P(None, ('seq', 'tp')), may hold values from -0.09375 to 0.09375
- down_weight: bfloat16 [7168, 3584], P('tp'), may hold values from -0.0625 to 0.0625
- next_weight: bfloat16 [3584, 8192], P(None, 'tp'), may hold values from -0.09375 to 0.09375
- post_attn_gain: float32 [3584], replicated, may hold values from 0.1 to 1.9
- pre_ffw_gain: float32 [3584], replicated, may hold values from 0.1 to 1.9
- post_ffw_gain: float32 [3584], replicated, may hold values from 0.1 to 1.9
- next_gain: float32 [3584], replicated, may hold values from 0.1 to 1.9
Outputs:
- next_qkv: bfloat16 [6144, 8192], P('seq', 'tp')
The draws below stay inside these ranges and needn't reach their ends.
Inputs may be any that keep to these rules, and one draw needn't show every extreme that they name: The lengths of 4 prompts laid end to end; they sum to 6144 and the longest is exactly 3072.
All inputs are finite; a program needn't handle non-finite values.
Results may differ from the reference program's by a relative error of at most 0.022.
Values may be sent and summed in bfloat16 or wider, within the bound.
A program may use at most 192 MiB of HBM per device.

```python
import math
import jax
import jax.numpy as jnp
import numpy as np
from jax import lax

D = 3584
HEADS = 16
KV_HEADS = 8
HEAD_DIM = 256
FFW = 7168
PROMPTS = 4
TOK_DEV = 384
TOKENS = 6144
MOST = 3072
QKV_COLS = 8192


def draw_hidden_in(key, part):
    key_base, key_rows, key_cols = jax.random.split(key, 3)
    base = jnp.clip(jax.random.normal(key_base, (TOKENS, D), jnp.float32), -4.0, 4.0)
    row_scale = jnp.exp(jax.random.uniform(key_rows, (TOKENS, 1), jnp.float32, -1.15, 1.15))
    col_scale = jnp.exp(jax.random.uniform(key_cols, (1, D), jnp.float32, -1.15, 1.15))
    return (base * row_scale * col_scale).astype(jnp.bfloat16)


def draw_joined_inputs(key, part):
    per_group = HEADS // KV_HEADS
    group_cols = (per_group + 2) * HEAD_DIM
    key_base, key_rows = jax.random.split(key, 2)
    base = jnp.clip(jax.random.normal(key_base, (TOKENS, KV_HEADS, group_cols), jnp.float32), -4.0, 4.0)
    row_scale = jnp.exp(jax.random.uniform(key_rows, (TOKENS, 1, 1), jnp.float32, -1.15, 1.15))
    lanes = jnp.arange(group_cols)[None, None, :]
    base = jnp.where(lanes >= (per_group + 1) * HEAD_DIM, base * row_scale, base)
    return base.reshape(TOKENS, KV_HEADS * group_cols).astype(jnp.bfloat16)


def block_scale(rng, shape, shards, low, top_value):
    def one(axis_at, blocks):
        steps = jax.random.uniform(jax.random.fold_in(jax.random.fold_in(rng, 6), axis_at), (blocks,), jnp.float32, low / len(shards), top_value / len(shards))
        return jnp.repeat(jnp.exp(steps), shape[axis_at] // blocks).reshape((-1,) + (1,) * (len(shape) - axis_at - 1))

    loudness = one(*shards[0])
    for cut in shards[1:]:
        loudness = loudness * one(*cut)
    return loudness


def length_profile(count, total, most, skew):
    portions = [(1 << 20) // math.isqrt(rank ** skew) + 1 for rank in range(2, count + 1)]
    rest, counts = total - most - (count - 1), [1] * (count - 1)
    while rest > 0:
        movable = [i for i in range(count - 1) if counts[i] < most]
        pool, left = sum([portions[i] for i in movable]), rest
        for i in movable:
            addition = min(most - counts[i], max(1, left * portions[i] // pool), rest)
            counts[i] = counts[i] + addition
            rest = rest - addition
    return np.array([most] + counts)


def ragged_sizes(stream_key, count, total, limit, skew):
    if count == 2:
        one = jax.random.randint(stream_key, (), max(1, total - limit), min(limit, total - 1) + 1)
        return jnp.stack([one, total - one])
    tallies = jnp.asarray(length_profile(count, total, limit, skew), jnp.int32)
    pairs = (count - 1) // 2
    donor, receiver = tallies[1:1 + 2 * pairs:2], tallies[2:2 + 2 * pairs:2]
    slack = jnp.minimum(donor - 1, limit - receiver)
    moved = jax.random.randint(jax.random.fold_in(stream_key, 1), (pairs,), 0, 1 << 20) % (slack + 1)
    tallies = tallies.at[1:1 + 2 * pairs:2].set(donor - moved).at[2:2 + 2 * pairs:2].set(receiver + moved)
    return tallies[jax.random.permutation(jax.random.fold_in(stream_key, 2), count)]


def gaussian(key, dims, deviation, reach, cuts=(), held_as=jnp.bfloat16):
    values = jax.random.normal(key, dims, jnp.float32) * deviation
    if len(cuts) > 0:
        values = block_scale(key, dims, cuts, -0.22, 0.18) * values
    return jnp.clip(values, min=-reach, max=reach).astype(held_as)


def setup_inputs(seed: int = 0) -> dict:
    seeds = jax.random.split(jax.random.key(seed), 12)
    return {
        "hidden_in": draw_hidden_in(jax.random.fold_in(seeds[11], 71), 0),
        "joined_inputs": draw_joined_inputs(jax.random.fold_in(seeds[11], 71), 0),
        "lengths": ragged_sizes(seeds[2], PROMPTS, TOKENS, MOST, 2).astype(jnp.int32),
        "o_weight": gaussian(seeds[3], (HEADS * HEAD_DIM, D), (HEADS * HEAD_DIM) ** -0.5, 0.09375, ((0, 8),)),
        "gate_up": gaussian(seeds[4], (2, D, FFW), D ** -0.5, 0.09375, ((1, 128),), jnp.float32),
        "down_weight": gaussian(seeds[5], (FFW, D), FFW ** -0.5, 0.0625, ((0, 8),)),
        "next_weight": gaussian(seeds[6], (D, QKV_COLS), D ** -0.5, 0.09375, ((1, 8),)),
        "post_attn_gain": jnp.clip(1.0 + 0.18 * jax.random.normal(seeds[7], (D,), jnp.float32), 0.1, 1.9),
        "pre_ffw_gain": jnp.clip(1.0 + 0.18 * jax.random.normal(seeds[8], (D,), jnp.float32), 0.1, 1.9),
        "post_ffw_gain": jnp.clip(1.0 + 0.18 * jax.random.normal(seeds[9], (D,), jnp.float32), 0.1, 1.9),
        "next_gain": jnp.clip(1.0 + 0.18 * jax.random.normal(seeds[10], (D,), jnp.float32), 0.1, 1.9),
    }


def rms_norm(values, gain):
    meansq = lax.optimization_barrier(jnp.mean(values * values, axis=-1, keepdims=True))
    return values * lax.rsqrt(meansq + 1e-06) * gain.astype(jnp.float32)

def reference(hidden_in, joined_inputs, lengths, o_weight, gate_up, down_weight, next_weight, post_attn_gain, pre_ffw_gain, post_ffw_gain, next_gain):
    per_group = HEADS // KV_HEADS
    group_cols = (per_group + 2) * HEAD_DIM
    grouped = joined_inputs.reshape(TOKENS, KV_HEADS, group_cols)
    queries = grouped[:, :, :per_group * HEAD_DIM].reshape(TOKENS, KV_HEADS, per_group, HEAD_DIM).astype(jnp.float32)
    keys_all = grouped[:, :, per_group * HEAD_DIM:(per_group + 1) * HEAD_DIM].astype(jnp.float32)
    values_all = grouped[:, :, (per_group + 1) * HEAD_DIM:].astype(jnp.float32)
    ends = jnp.cumsum(lengths).astype(jnp.int32)
    places = jnp.arange(TOKENS, dtype=jnp.int32)
    prompt_ids = lax.optimization_barrier(jnp.sum((places[:, None] >= ends[None, :]).astype(jnp.int32), axis=1))

    def attend_block(block_index):
        first_row = (block_index * TOK_DEV).astype(jnp.int32)
        query_block = lax.dynamic_slice_in_dim(queries, first_row, TOK_DEV, 0)
        query_place = first_row + jnp.arange(TOK_DEV, dtype=jnp.int32)
        query_ids = lax.dynamic_slice_in_dim(prompt_ids, first_row, TOK_DEV, 0)
        scores = jnp.einsum('qgrd,kgd->qgrk', query_block, keys_all) * HEAD_DIM ** (-0.5)
        allowed = (query_ids[:, None] == prompt_ids[None, :]) & (places[None, :] <= query_place[:, None])
        allowed = allowed[:, None, None, :]
        scores = jnp.where(allowed, scores, -jnp.inf)
        peak = lax.optimization_barrier(jnp.max(scores, axis=-1, keepdims=True))
        weights = jnp.where(allowed, jnp.exp(scores - peak), 0.0)
        norm_sum = lax.optimization_barrier(jnp.sum(weights, axis=-1))
        rounded = lax.optimization_barrier(weights.astype(jnp.bfloat16)).astype(jnp.float32)
        blended = jnp.einsum('qgrk,kgd->qgrd', rounded, values_all) / norm_sum[..., None]
        return blended.astype(jnp.bfloat16).reshape(TOK_DEV, HEADS * HEAD_DIM)
    attended = lax.map(attend_block, jnp.arange(TOKENS // TOK_DEV, dtype=jnp.int32)).reshape(TOKENS, HEADS * HEAD_DIM)
    projected = jnp.dot(attended, o_weight, preferred_element_type=jnp.float32)
    residual_mid = hidden_in.astype(jnp.float32) + rms_norm(projected, post_attn_gain)
    ffw_in = rms_norm(residual_mid, pre_ffw_gain).astype(jnp.bfloat16)
    server_gate_up = gate_up.astype(jnp.bfloat16)
    gate = jnp.dot(ffw_in, server_gate_up[0], preferred_element_type=jnp.float32)
    up_part = jnp.dot(ffw_in, server_gate_up[1], preferred_element_type=jnp.float32)
    activated = (jax.nn.gelu(gate, approximate=True) * up_part).astype(jnp.bfloat16)
    ffw_out = jnp.dot(activated, down_weight, preferred_element_type=jnp.float32)
    residual_out = residual_mid + rms_norm(ffw_out, post_ffw_gain)
    next_in = rms_norm(residual_out, next_gain).astype(jnp.bfloat16)
    return jnp.dot(next_in, next_weight, preferred_element_type=jnp.float32).astype(jnp.bfloat16)
```

```python
import jax
import jax.numpy as jnp
from jax import lax
from jax.sharding import PartitionSpec as P

HEADS = 16
KV_HEADS = 8
HEAD_DIM = 256


def rms_norm(values, gain):
    meansq = jnp.mean(values * values, axis=-1, keepdims=True)
    return values * lax.rsqrt(meansq + 1e-06) * gain


def local(
    hidden_in,
    joined_inputs,
    lengths,
    o_weight,
    gate_up,
    down_weight,
    next_weight,
    post_attn_gain,
    pre_ffw_gain,
    post_ffw_gain,
    next_gain,
):
    tp_count = lax.axis_size("tp")
    row_count = hidden_in.shape[0]
    per_group = HEADS // KV_HEADS
    group_cols = (per_group + 2) * HEAD_DIM
    local_groups = joined_inputs.shape[1] // group_cols
    grouped = joined_inputs.reshape(row_count, local_groups, group_cols)
    queries = grouped[:, :, : per_group * HEAD_DIM].reshape(
        row_count, local_groups, per_group, HEAD_DIM
    )
    own_keys = grouped[:, :, per_group * HEAD_DIM : (per_group + 1) * HEAD_DIM]
    own_values = grouped[:, :, (per_group + 1) * HEAD_DIM :]
    keys_all, values_all = (
        lax.all_gather(own_keys, "seq", axis=0, tiled=True),
        lax.all_gather(own_values, "seq", axis=0, tiled=True),
    )
    total_rows = keys_all.shape[0]
    seq_index = lax.axis_index("seq")
    position = seq_index * row_count
    ends = jnp.cumsum(lengths)
    places = jnp.arange(total_rows, dtype=jnp.int32)
    prompt_ids = jnp.sum((places[:, None] >= ends[None, :]).astype(jnp.int32), axis=1)
    query_place = position + jnp.arange(row_count, dtype=jnp.int32)
    query_ids = lax.dynamic_slice_in_dim(prompt_ids, position, row_count, 0)
    scale = HEAD_DIM ** (-0.5)
    scores = (
        jnp.einsum("qgrd,kgd->qgrk", queries, keys_all, preferred_element_type=jnp.float32) * scale
    )
    allowed = (
        (query_ids[:, None] == prompt_ids[None, :]) & (places[None, :] <= query_place[:, None])
    )[:, None, None, :]
    scores = jnp.where(allowed, scores, -jnp.inf)
    peak = jnp.max(scores, axis=-1, keepdims=True)
    weights = jnp.where(allowed, jnp.exp(scores - peak), 0.0)
    norm_sum = jnp.sum(weights, axis=-1)
    blended = jnp.einsum(
        "qgrk,kgd->qgrd",
        weights.astype(jnp.bfloat16),
        values_all,
        preferred_element_type=jnp.float32,
    )
    blended = blended / norm_sum[..., None]
    attended = blended.astype(jnp.bfloat16).reshape(row_count, local_groups * per_group * HEAD_DIM)
    projected = jnp.dot(attended, o_weight, preferred_element_type=jnp.float32)

    tp_index = lax.axis_index("tp")
    slice_rows = row_count // tp_count

    def scattered(values):
        return lax.psum_scatter(
            values.astype(jnp.bfloat16), "tp", scatter_dimension=0, tiled=True
        ).astype(jnp.float32)

    own_hidden = lax.dynamic_slice_in_dim(hidden_in, tp_index * slice_rows, slice_rows, 0)
    residual_mid = own_hidden.astype(jnp.float32) + rms_norm(scattered(projected), post_attn_gain)
    ffw_in = rms_norm(residual_mid, pre_ffw_gain).astype(jnp.bfloat16)
    ffw_in = lax.all_gather(ffw_in, "tp", axis=0, tiled=True)
    server_low = gate_up.astype(jnp.bfloat16)
    unit_rows = lax.all_to_all(server_low, "tp", split_axis=2, concat_axis=1, tiled=True)
    local_units = lax.all_gather(unit_rows, "seq", axis=1, tiled=True)
    gate = jnp.dot(ffw_in, local_units[0], preferred_element_type=jnp.float32)
    up_part = jnp.dot(ffw_in, local_units[1], preferred_element_type=jnp.float32)
    activated = (jax.nn.gelu(gate, approximate=True) * up_part).astype(jnp.bfloat16)
    ffw_out = jnp.dot(activated, down_weight, preferred_element_type=jnp.float32)
    residual_out = residual_mid + rms_norm(scattered(ffw_out), post_ffw_gain)
    next_in = rms_norm(residual_out, next_gain).astype(jnp.bfloat16)
    next_in = lax.all_gather(next_in, "tp", axis=0, tiled=True)
    return jnp.dot(next_in, next_weight, preferred_element_type=jnp.float32).astype(jnp.bfloat16)


def solution(mesh):
    in_specs = (
        P("seq", None),
        P("seq", "tp"),
        P(),
        P("tp", None),
        P(None, ("seq", "tp"), None),
        P("tp", None),
        P(None, "tp"),
        P(),
        P(),
        P(),
        P(),
    )
    out_specs = P("seq", "tp")
    return jax.shard_map(local, mesh=mesh, in_specs=in_specs, out_specs=out_specs, check_vma=False)
```

```python
import jax
import jax.numpy as jnp
from jax import lax
from jax.experimental import pallas as pl
from jax.experimental.pallas import tpu as pltpu
from jax.sharding import PartitionSpec as P

MESH = pl.DeviceIdType.MESH
BF = jnp.bfloat16
F32 = jnp.float32
D = 3584
HALF = D // 2
ROWS = 384
HD = 256
UNITS = 896
PIECE = 28
CHUNK = 224
BLK = 48
GROUP = 192
QKV = 1024
NEG = -1e30


def al(value, to):
    return pl.multiple_of(value, to)


def kernel(
    lens, hid, joined, ow, gu, dw, nw, g_attn, g_pre, g_post, g_next,
    out,
    qbuf, kvbuf, owv, dwv, nwv, hidv, guv, gub, abuf, wbuf,
    mbuf, lbuf, acc, att, pb1, pb2, r1, r2, rx, sx, ag1, ag2, act, resid,
    lsem, kv_s, kv_r, a_s, a_r, w_s, w_r, r1_r, r2_r, rx_r, rs_s, ag_s, ag_r,
):
    s = lax.axis_index("seq")
    t = lax.axis_index("tp")
    x = s // 8
    z = (s // 2) % 4
    c = s % 2
    y = t // 2
    h = t % 2
    o = 1 - h

    def dev_seq(xx, zz, cc):
        return (xx * 8 + zz * 2 + cc, t)

    def dev_tp(yy, hh):
        return (s, yy * 2 + hh)

    zp, zm = (z + 1) % 4, (z + 3) % 4
    yp, ym, y2 = (y + 1) % 4, (y + 3) % 4, (y + 2) % 4
    sib = dev_seq(x, z, 1 - c)
    xnb = dev_seq(1 - x, z, c)
    zup = dev_seq(x, zp, c)
    zdn = dev_seq(x, zm, c)
    yup = dev_tp(yp, h)
    ydn = dev_tp(ym, h)
    xhi = dev_tp(y, o)

    barrier = pltpu.get_barrier_semaphore()
    tp_peers = [(s, (t + k) % 8) for k in range(1, 8)]
    for peer in [sib, xnb, zup, zdn] + tp_peers:
        pl.semaphore_signal(barrier, inc=1, device_id=peer, device_id_type=MESH)

    own_block = h * 4 + y
    loads = [
        (joined.at[:, pl.ds(512, 512)], kvbuf.at[s]),
        (joined.at[:, pl.ds(0, 256)], qbuf.at[0]),
        (joined.at[:, pl.ds(256, 256)], qbuf.at[1]),
        (gu, guv),
        (ow, owv),
        (hid.at[pl.ds(al(own_block * BLK, 16), BLK), :], hidv),
        (dw, dwv),
        (nw, nwv),
    ]
    local_copies = [
        pltpu.make_async_copy(src, dst, lsem.at[i]) for i, (src, dst) in enumerate(loads)
    ]
    for copy in local_copies:
        copy.start()

    def rcopy(src, dst, send, recv, dev):
        return pltpu.make_async_remote_copy(
            src_ref=src,
            dst_ref=dst,
            send_sem=send,
            recv_sem=recv,
            device_id=dev,
            device_id_type=MESH,
        )

    pl.semaphore_wait(barrier, 11)

    def kv_send(slot, dev, sem):
        return rcopy(kvbuf.at[slot], kvbuf.at[slot], kv_s.at[sem], kv_r.at[slot], dev)

    def kv_arrived(slot):
        kv_send(slot, sib, 0).wait_recv()

    kv_sent = []

    def kv_go(cond, slot, dev):
        sem = len(kv_sent)
        kv_sent.append((cond, slot, dev))

        @pl.when(cond)
        def _():
            kv_send(slot, dev, sem).start()

    local_copies[0].wait()
    always = s >= 0
    kv_go(z < 3, s, zup)
    kv_go(x == 0, s, xnb)
    kv_go(z == 0, s, zdn)
    kv_go(c == 0, s, sib)

    local_copies[3].wait()
    for k in range(8):
        gub[k] = guv[:, :, k * UNITS : (k + 1) * UNITS].astype(BF)

    def a_send(k):
        peer = (t + k) % 8
        return rcopy(gub.at[peer], abuf.at[t], a_s.at[k], a_r.at[k], (s, peer))

    for k in range(1, 8):
        a_send(k).start()

    local_copies[1].wait()
    local_copies[2].wait()
    mbuf[...] = jnp.full(mbuf.shape, NEG, F32)
    lbuf[...] = jnp.zeros(lbuf.shape, F32)
    acc[...] = jnp.zeros(acc.shape, F32)

    end0 = lens[0]
    end1 = end0 + lens[1]
    end2 = end1 + lens[2]

    def flash(slot):
        place = s * ROWS + lax.broadcasted_iota(jnp.int32, (ROWS, 1), 0)
        low = jnp.where(
            place >= end2,
            end2,
            jnp.where(place >= end1, end1, jnp.where(place >= end0, end0, 0)),
        )
        other = slot * ROWS + lax.broadcasted_iota(jnp.int32, (ROWS, ROWS), 1)
        allowed = (other >= low) & (other <= place)

        def head(r, carry):
            scores = lax.dot_general(
                qbuf[r],
                kvbuf[slot, :, 0:HD],
                (((1,), (1,)), ((), ())),
                preferred_element_type=F32,
            ) * (HD ** -0.5)
            scores = jnp.where(allowed, scores, NEG)
            before = mbuf[r]
            peak = jnp.maximum(before, jnp.max(scores, axis=-1, keepdims=True))
            weights = jnp.exp(scores - peak)
            fade = jnp.exp(before - peak)
            lbuf[r] = lbuf[r] * fade + jnp.sum(weights, axis=-1, keepdims=True)
            mbuf[r] = peak
            acc[r] = acc[r] * fade + jnp.dot(
                weights.astype(BF), kvbuf[slot, :, HD : 2 * HD], preferred_element_type=F32
            )
            return carry

        lax.fori_loop(0, 2, head, 0)

    def up_ok(off):
        return z + off >= 0

    def down_ok(off):
        return (x == 1) & (z + off <= 3)

    def up_slot(off, core):
        return x * 8 + (z + off + 4) % 4 * 2 + core

    def down_slot(off, core):
        return (z + off) % 4 * 2 + core

    def w_ref(slot, m):
        return wbuf.at[m, pl.ds(al(slot * CHUNK, 16), CHUNK), :]

    w_sent = []

    def w_copy(slot, m, dev, sem):
        return rcopy(w_ref(slot, m), w_ref(slot, m), w_s.at[sem], w_r.at[slot, m], dev)

    def w_go(slot, m, dev):
        w_copy(slot, m, dev, len(w_sent)).start()
        w_sent.append((slot, m, dev))

    def w_arrived(slot, m):
        w_copy(slot, m, sib, 0).wait_recv()

    def repack():
        for k in range(1, 8):
            peer = (t + 8 - k) % 8
            rcopy(gub.at[0], abuf.at[peer], a_s.at[k], a_r.at[k], (s, peer)).wait_recv()
        abuf[t] = gub[t]
        for m in range(2):
            rows = jnp.concatenate([abuf[k, m].astype(F32) for k in range(8)], axis=0)
            wbuf[m, pl.ds(al(s * CHUNK, 16), CHUNK), :] = rows.astype(BF)

    def comm_of(entries):
        plan = []
        for cond, slot, forward, relays in entries:
            sends = [(cond if forward is None else cond & forward, sib)] + relays
            numbered = []
            for ok, dev in sends:
                numbered.append((ok, dev, len(kv_sent)))
                kv_sent.append((ok, slot, dev))
            plan.append((cond, slot, numbered))

        def run():
            for cond, slot, numbered in plan:

                @pl.when(cond)
                def _(slot=slot):
                    kv_arrived(slot)

                for ok, dev, sem in numbered[1:] + numbered[:1]:

                    @pl.when(ok)
                    def _(slot=slot, dev=dev, sem=sem):
                        kv_send(slot, dev, sem).start()

        return run

    middle = (z == 1) | (z == 2)
    comm_a = comm_of([
        (up_ok(-1), up_slot(-1, c), None, [(middle, zup)]),
        (down_ok(0), down_slot(0, c), c == 1, [((x == 1) & (z >= 1), zdn), ((x == 1) & (z == 3), zup)]),
    ])
    comm_b = comm_of([
        (down_ok(1), down_slot(1, c), None, [((x == 1) & middle, zdn)]),
        (up_ok(-3), up_slot(-3, c), None, []),
        (down_ok(3), down_slot(3, c), None, []),
    ])
    comm_c = comm_of([
        (up_ok(-2), up_slot(-2, c), None, []),
        (down_ok(2), down_slot(2, c), None, []),
    ])

    offsets = {2: -1, 3: 0, 4: -1, 5: 0, 6: 1, 7: -3, 8: 3, 9: 1, 10: -3, 11: 3, 12: -2, 13: 2, 14: -2, 15: 2}

    def step(i, carry):
        @pl.when(i == 2)
        def _():
            comm_a()

        @pl.when(i == 6)
        def _():
            comm_b()

        @pl.when(i == 12)
        def _():
            comm_c()

        off = 0
        for k, value in offsets.items():
            off = off + jnp.where(i == k, value, 0)
        from_sib = (i == 1) | (i == 4) | (i == 5) | ((i >= 9) & (i <= 11)) | (i >= 14)
        is_down = (i >= 2) & (off >= 0)
        column = jnp.where(is_down, 0, x)
        zz = z + off
        ok = jnp.where(is_down, (x == 1) & (zz <= 3), zz >= 0)
        ok = ok & ((i != 1) | (c == 1)) & ((i != 5) | (c == 0))
        core = jnp.where(from_sib, 1 - c, c)
        slot = column * 8 + (zz + 4) % 4 * 2 + core

        @pl.when(ok & from_sib)
        def _():
            kv_arrived(slot)

        @pl.when(ok)
        def _():
            flash(slot)

        return carry

    lax.fori_loop(0, 16, step, 0)

    repack()
    for r in range(2):
        att[:, r * HD : (r + 1) * HD] = (acc[r] / lbuf[r, :, 0:1]).astype(BF)

    for m in range(2):
        w_go(s, m, xnb)
    w_go(s, 0, zup)
    w_go(s, 1, zdn)
    w_go(s, 1, zup)
    w_go(s, 0, zdn)
    for m in range(2):
        w_go(s, m, sib)

    s_x = (1 - x) * 8 + z * 2 + c
    s_zm = x * 8 + zm * 2 + c
    s_zp = x * 8 + zp * 2 + c
    s_z2 = x * 8 + (z + 2) % 4 * 2 + c
    s_xzm = (1 - x) * 8 + zm * 2 + c
    s_xzp = (1 - x) * 8 + zp * 2 + c
    s_xz2 = (1 - x) * 8 + (z + 2) % 4 * 2 + c

    def w_stage1():
        w_arrived(s_zm, 0)
        w_go(s_zm, 0, zup)
        w_arrived(s_zp, 1)
        w_go(s_zp, 1, zdn)
        for m in range(2):
            w_arrived(s_x, m)
        w_go(s_x, 0, zup)
        w_go(s_x, 1, zdn)
        w_go(s_x, 1, zup)
        w_go(s_x, 0, zdn)
        w_arrived(s_zm, 1)
        w_arrived(s_zp, 0)
        for slot in (s_x, s_zm, s_zp):
            for m in range(2):
                w_go(slot, m, sib)

    def w_stage2():
        for m in range(2):
            w_arrived(s_z2, m)
            w_go(s_z2, m, xnb)
            w_go(s_z2, m, sib)

    def w_stage3():
        for slot in (s_xzm, s_xzp):
            for m in range(2):
                w_arrived(slot, m)
                w_go(slot, m, sib)

    def w_stage4():
        for m in range(2):
            w_arrived(s_xz2, m)
            w_go(s_xz2, m, sib)

    def w_stage5():
        for xx in range(2):
            for zz in range(4):
                for m in range(2):
                    w_arrived(xx * 8 + zz * 2 + 1 - c, m)

    rs_sent = []

    def send(src, dst, recv, dev):
        copy = rcopy(src, dst, rs_s.at[len(rs_sent)], recv, dev)
        copy.start()
        rs_sent.append(copy)

    def rows_of(block):
        return pl.ds(al(block * BLK, 16), BLK)

    cols = (pl.ds(0, HALF), pl.ds(HALF, HALF))
    phase_h = (o, h)

    def rs_start(k, pb, p):
        g = phase_h[p]
        far = rows_of(g * 4 + y2)
        send(pb.at[far, cols[0]], r1.at[k, p, 0], r1_r.at[k, p, 0], yup)
        send(pb.at[far, cols[1]], r1.at[k, p, 1], r1_r.at[k, p, 1], ydn)
        send(pb.at[rows_of(g * 4 + yp), cols[1]], r2.at[k, p, 0, 1], r2_r.at[k, p, 0, 1], yup)
        send(pb.at[rows_of(g * 4 + ym), cols[0]], r2.at[k, p, 1, 0], r2_r.at[k, p, 1, 0], ydn)

    def rs_middle(k, pb, p):
        g = phase_h[p]
        for way, (yy, dev) in enumerate(((yp, yup), (ym, ydn))):
            near = rows_of(g * 4 + yy)
            rcopy(r1.at[k, p, way], r1.at[k, p, way], rs_s.at[0], r1_r.at[k, p, way], dev).wait_recv()
            pb[near, cols[way]] = (
                pb[near, cols[way]].astype(F32) + r1[k, p, way].astype(F32)
            ).astype(BF)
            send(pb.at[near, cols[way]], r2.at[k, p, way, way], r2_r.at[k, p, way, way], dev)

    def rs_end(k, pb, p):
        g = phase_h[p]
        for way in range(2):
            for half in range(2):
                ref = r2.at[k, p, way, half]
                rcopy(ref, ref, rs_s.at[0], r2_r.at[k, p, way, half], yup).wait_recv()
        mine = rows_of(g * 4 + y)
        return jnp.concatenate(
            [
                pb[mine, cols[half]].astype(F32)
                + r2[k, p, 0, half].astype(F32)
                + r2[k, p, 1, half].astype(F32)
                for half in range(2)
            ],
            axis=1,
        )

    def rs_cross(k, pb):
        sx[k] = rs_end(k, pb, 0).astype(BF)
        send(sx.at[k], rx.at[k], rx_r.at[k], xhi)

    def rs_total(k, pb):
        total = rs_end(k, pb, 1)
        rcopy(rx.at[k], rx.at[k], rs_s.at[0], rx_r.at[k], xhi).wait_recv()
        return total + rx[k].astype(F32)

    def normed(values, gain):
        meansq = jnp.mean(values * values, axis=-1, keepdims=True)
        return values * lax.rsqrt(meansq + 1e-06) * gain[...]

    ag_sent = []

    def ag_copy(k, ag, block, half, dev, sem):
        ref = ag.at[rows_of(block), cols[half]]
        return rcopy(ref, ref, ag_s.at[sem], ag_r.at[k, block, half], dev)

    def ag_go(k, ag, block, half, dev):
        copy = ag_copy(k, ag, block, half, dev, len(ag_sent))
        copy.start()
        ag_sent.append(copy)

    def ag_arrived(k, ag, block, half):
        ag_copy(k, ag, block, half, xhi, 0).wait_recv()

    def ag_start(k, ag):
        b = h * 4 + y
        ag_go(k, ag, b, 0, xhi)
        ag_go(k, ag, b, 1, xhi)
        ag_go(k, ag, b, 0, yup)
        ag_go(k, ag, b, 1, ydn)
        ag_go(k, ag, b, 1, yup)
        ag_go(k, ag, b, 0, ydn)

    def ag_relay(k, ag, g):
        ag_arrived(k, ag, g * 4 + ym, 0)
        ag_go(k, ag, g * 4 + ym, 0, yup)
        ag_arrived(k, ag, g * 4 + yp, 1)
        ag_go(k, ag, g * 4 + yp, 1, ydn)

    def ag_cross(k, ag):
        b = o * 4 + y
        for half in range(2):
            ag_arrived(k, ag, b, half)
        ag_go(k, ag, b, 0, yup)
        ag_go(k, ag, b, 1, ydn)
        ag_go(k, ag, b, 1, yup)
        ag_go(k, ag, b, 0, ydn)

    def ag_end(k, ag, g):
        ag_arrived(k, ag, g * 4 + ym, 1)
        ag_arrived(k, ag, g * 4 + yp, 0)
        ag_arrived(k, ag, g * 4 + y2, 0)
        ag_arrived(k, ag, g * 4 + y2, 1)

    def group_rows(g):
        return pl.ds(al(g * GROUP, 16), GROUP)

    def project(lhs, weight, g, pb):
        def tile(j, carry):
            at = pl.ds(al(j * 256, 256), 256)
            pb[group_rows(g), at] = jnp.dot(
                lhs[group_rows(g), :], weight[:, at], preferred_element_type=F32
            ).astype(BF)
            return carry

        lax.fori_loop(0, D // 256, tile, 0)

    local_copies[4].wait()
    project(att, owv, o, pb1)
    rs_start(0, pb1, 0)
    project(att, owv, h, pb1)
    rs_start(0, pb1, 1)
    rs_middle(0, pb1, 0)
    rs_middle(0, pb1, 1)
    rs_cross(0, pb1)
    local_copies[5].wait()
    w_stage1()
    total = rs_total(0, pb1)
    mid = hidv[...].astype(F32) + normed(total, g_attn)
    resid[...] = mid
    ag1[rows_of(own_block), :] = normed(mid, g_pre).astype(BF)
    ag_start(0, ag1)
    ag_relay(0, ag1, h)
    ag_cross(0, ag1)
    w_stage2()
    ag_end(0, ag1, h)
    ag_relay(0, ag1, o)
    w_stage3()
    w_stage4()
    w_stage5()

    def ffn(g):
        def tile(j, carry):
            at = pl.ds(al(j * 128, 128), 128)
            both = jnp.concatenate([wbuf[0, :, at], wbuf[1, :, at]], axis=1)
            joint = jnp.dot(ag1[group_rows(g), :], both, preferred_element_type=F32)
            gate = joint[:, :128]
            up = joint[:, 128:]
            inner = 0.7978845608028654 * (gate + 0.044715 * (gate * gate * gate))
            act[group_rows(g), at] = (0.5 * gate * (1.0 + jnp.tanh(inner)) * up).astype(BF)
            return carry

        lax.fori_loop(0, UNITS // 128, tile, 0)

    ffn(h)
    ag_end(0, ag1, o)
    ffn(o)
    local_copies[6].wait()
    project(act, dwv, o, pb2)
    rs_start(1, pb2, 0)
    project(act, dwv, h, pb2)
    rs_start(1, pb2, 1)
    rs_middle(1, pb2, 0)
    rs_middle(1, pb2, 1)
    rs_cross(1, pb2)
    total = rs_total(1, pb2)
    last = resid[...] + normed(total, g_post)
    ag2[rows_of(own_block), :] = normed(last, g_next).astype(BF)
    ag_start(1, ag2)
    ag_relay(1, ag2, h)
    ag_cross(1, ag2)
    ag_end(1, ag2, h)
    ag_relay(1, ag2, o)
    local_copies[7].wait()

    def next_qkv(g):
        def tile(j, carry):
            at = pl.ds(al(j * 256, 256), 256)
            out[group_rows(g), at] = jnp.dot(
                ag2[group_rows(g), :], nwv[:, at], preferred_element_type=F32
            ).astype(BF)
            return carry

        lax.fori_loop(0, QKV // 256, tile, 0)

    next_qkv(h)
    ag_end(1, ag2, o)
    next_qkv(o)

    for sem, (cond, slot, dev) in enumerate(kv_sent):

        @pl.when(cond)
        def _(slot=slot, dev=dev, sem=sem):
            kv_send(slot, dev, sem).wait_send()

    for k in range(1, 8):
        a_send(k).wait_send()
    for sem, (slot, m, dev) in enumerate(w_sent):
        w_copy(slot, m, dev, sem).wait_send()
    for copy in rs_sent + ag_sent:
        copy.wait_send()


def local(hid, joined, lengths, ow, gu, dw, nw, g_attn, g_pre, g_post, g_next):
    hbm = pl.BlockSpec(memory_space=pl.ANY)
    vmem = pl.BlockSpec(memory_space=pltpu.VMEM)
    smem = pl.BlockSpec(memory_space=pltpu.SMEM)
    V = pltpu.VMEM
    DMA = pltpu.SemaphoreType.DMA
    scratch = [
        V((2, ROWS, HD), BF),
        V((16, ROWS, 2 * HD), BF),
        V(ow.shape, BF),
        V(dw.shape, BF),
        V(nw.shape, BF),
        V((BLK, D), BF),
        V(gu.shape, F32),
        V((8, 2, PIECE, UNITS), BF),
        V((8, 2, PIECE, UNITS), BF),
        V((2, D, UNITS), BF),
        V((2, ROWS, 1), F32),
        V((2, ROWS, 1), F32),
        V((2, ROWS, HD), F32),
        V((ROWS, 2 * HD), BF),
        V((ROWS, D), BF),
        V((ROWS, D), BF),
        V((2, 2, 2, BLK, HALF), BF),
        V((2, 2, 2, 2, BLK, HALF), BF),
        V((2, BLK, D), BF),
        V((2, BLK, D), BF),
        V((ROWS, D), BF),
        V((ROWS, D), BF),
        V((ROWS, UNITS), BF),
        V((BLK, D), F32),
        DMA((8,)),
        DMA((24,)),
        DMA((16,)),
        DMA((8,)),
        DMA((8,)),
        DMA((48,)),
        DMA((16, 2)),
        DMA((2, 2, 2)),
        DMA((2, 2, 2, 2)),
        DMA((2,)),
        DMA((32,)),
        DMA((40,)),
        DMA((2, 8, 2)),
    ]
    return pl.pallas_call(
        kernel,
        out_shape=jax.ShapeDtypeStruct((ROWS, QKV), BF),
        in_specs=[smem, hbm, hbm, hbm, hbm, hbm, hbm, vmem, vmem, vmem, vmem],
        out_specs=vmem,
        scratch_shapes=scratch,
        compiler_params=pltpu.CompilerParams(
            collective_id=0, has_side_effects=True, vmem_limit_bytes=67043328
        ),
    )(
        lengths, hid, joined, ow, gu, dw, nw,
        g_attn.reshape(1, D), g_pre.reshape(1, D), g_post.reshape(1, D), g_next.reshape(1, D),
    )


def solution(mesh):
    in_specs = (
        P("seq", None),
        P("seq", "tp"),
        P(),
        P("tp", None),
        P(None, ("seq", "tp"), None),
        P("tp", None),
        P(None, "tp"),
        P(),
        P(),
        P(),
        P(),
    )
    return jax.shard_map(
        local, mesh=mesh, in_specs=in_specs, out_specs=P("seq", "tp"), check_vma=False
    )
```

```python
import jax
import jax.numpy as jnp
from jax import lax
from jax.experimental import pallas as pl
from jax.experimental.pallas import tpu as pltpu
from jax.sharding import PartitionSpec as P

MESH = pl.DeviceIdType.MESH
BF = jnp.bfloat16
F32 = jnp.float32
D = 3584
HALF = D // 2
ROWS = 384
HD = 256
UNITS = 896
PIECE = 28
CHUNK = 224
BLK = 48
GROUP = 192
QKV = 1024
NEG = -1e30


def al(value, to):
    return pl.multiple_of(value, to)


def kernel(
    lens, hid, joined, ow, gu, dw, nw, g_attn, g_pre, g_post, g_next,
    out,
    qbuf, kvbuf, owv, dwv, nwv, hidv, guv, gub, abuf, wbuf,
    mbuf, lbuf, acc, att, pb1, pb2, r1, r2, rx, sx, ag1, ag2, act, resid,
    lsem, kv_s, kv_r, a_s, a_r, w_s, w_r, r1_r, r2_r, rx_r, rs_s, ag_s, ag_r,
):
    s = lax.axis_index("seq")
    t = lax.axis_index("tp")
    x = s // 8
    z = (s // 2) % 4
    c = s % 2
    y = t // 2
    h = t % 2
    o = 1 - h

    def dev_seq(xx, zz, cc):
        return (xx * 8 + zz * 2 + cc, t)

    def dev_tp(yy, hh):
        return (s, yy * 2 + hh)

    zp, zm = (z + 1) % 4, (z + 3) % 4
    yp, ym, y2 = (y + 1) % 4, (y + 3) % 4, (y + 2) % 4
    sib = dev_seq(x, z, 1 - c)
    xnb = dev_seq(1 - x, z, c)
    zup = dev_seq(x, zp, c)
    zdn = dev_seq(x, zm, c)
    yup = dev_tp(yp, h)
    ydn = dev_tp(ym, h)
    xhi = dev_tp(y, o)

    barrier = pltpu.get_barrier_semaphore()
    tp_peers = [(s, (t + k) % 8) for k in range(1, 8)]
    for peer in [sib, xnb, zup, zdn] + tp_peers:
        pl.semaphore_signal(barrier, inc=1, device_id=peer, device_id_type=MESH)

    own_block = h * 4 + y
    loads = [
        (joined.at[:, pl.ds(512, 256)], kvbuf.at[s, 0]),
        (joined.at[:, pl.ds(0, 256)], qbuf.at[0]),
        (joined.at[:, pl.ds(256, 256)], qbuf.at[1]),
        (gu, guv),
        (ow, owv),
        (hid.at[pl.ds(al(own_block * BLK, 16), BLK), :], hidv),
        (dw, dwv),
        (nw, nwv),
        (joined.at[:, pl.ds(768, 256)], kvbuf.at[s, 1]),
    ]
    local_copies = [
        pltpu.make_async_copy(src, dst, lsem.at[i]) for i, (src, dst) in enumerate(loads)
    ]
    for copy in local_copies:
        copy.start()

    def rcopy(src, dst, send, recv, dev):
        return pltpu.make_async_remote_copy(
            src_ref=src,
            dst_ref=dst,
            send_sem=send,
            recv_sem=recv,
            device_id=dev,
            device_id_type=MESH,
        )

    pl.semaphore_wait(barrier, 11)

    def kv_send(slot, part, dev, sem):
        ref = kvbuf.at[slot, part]
        return rcopy(ref, ref, kv_s.at[sem], kv_r.at[slot, part], dev)

    def kv_arrived(slot, part):
        kv_send(slot, part, sib, 0).wait_recv()

    kv_sent = []
    for part in range(2):
        local_copies[(0, 8)[part]].wait()
        for ok, dev in ((z < 3, zup), (x == 0, xnb), (z == 0, zdn), (c == 0, sib)):
            sem = len(kv_sent)
            kv_sent.append((ok, s, part, dev))

            @pl.when(ok)
            def _(part=part, dev=dev, sem=sem):
                kv_send(s, part, dev, sem).start()

    local_copies[3].wait()
    for k in range(8):
        for m in range(2):
            gub[k, m] = guv[:, m, k * UNITS : (k + 1) * UNITS].astype(BF)

    def a_send(k):
        peer = (t + k) % 8
        return rcopy(gub.at[peer], abuf.at[t], a_s.at[k], a_r.at[k], (s, peer))

    for k in range(1, 8):
        a_send(k).start()

    local_copies[1].wait()
    local_copies[2].wait()
    mbuf[...] = jnp.full(mbuf.shape, NEG, F32)
    lbuf[...] = jnp.zeros(lbuf.shape, F32)
    acc[...] = jnp.zeros(acc.shape, F32)

    end0 = lens[0]
    end1 = end0 + lens[1]
    end2 = end1 + lens[2]

    def flash(slot):
        place = s * ROWS + lax.broadcasted_iota(jnp.int32, (ROWS, 1), 0)
        low = jnp.where(
            place >= end2,
            end2,
            jnp.where(place >= end1, end1, jnp.where(place >= end0, end0, 0)),
        )
        other = slot * ROWS + lax.broadcasted_iota(jnp.int32, (ROWS, ROWS), 1)
        allowed = (other >= low) & (other <= place)

        def head(r, carry):
            scores = lax.dot_general(
                qbuf[r],
                kvbuf[slot, 0],
                (((1,), (1,)), ((), ())),
                preferred_element_type=F32,
            ) * (HD ** -0.5)
            scores = jnp.where(allowed, scores, NEG)
            before = mbuf[r]
            peak = jnp.maximum(before, jnp.max(scores, axis=-1, keepdims=True))
            weights = jnp.exp(scores - peak)
            fade = jnp.exp(before - peak)
            lbuf[r] = lbuf[r] * fade + jnp.sum(weights, axis=-1, keepdims=True)
            mbuf[r] = peak
            acc[r] = acc[r] * fade + jnp.dot(
                weights.astype(BF), kvbuf[slot, 1], preferred_element_type=F32
            )
            return carry

        lax.fori_loop(0, 2, head, 0)

    def up_ok(off):
        return z + off >= 0

    def down_ok(off):
        return (x == 1) & (z + off <= 3)

    def up_slot(off, core):
        return x * 8 + (z + off + 4) % 4 * 2 + core

    def down_slot(off, core):
        return (z + off) % 4 * 2 + core

    def w_ref(slot, m):
        return wbuf.at[m, pl.ds(al(slot * CHUNK, 16), CHUNK), :]

    w_sent = []

    def w_copy(slot, m, dev, sem):
        return rcopy(w_ref(slot, m), w_ref(slot, m), w_s.at[sem], w_r.at[slot, m], dev)

    def w_go(slot, m, dev):
        w_copy(slot, m, dev, len(w_sent)).start()
        w_sent.append((slot, m, dev))

    def w_arrived(slot, m):
        w_copy(slot, m, sib, 0).wait_recv()

    def repack():
        for k in range(1, 8):
            peer = (t + 8 - k) % 8
            rcopy(gub.at[0], abuf.at[peer], a_s.at[k], a_r.at[k], (s, peer)).wait_recv()
        abuf[t] = gub[t]
        for m in range(2):
            rows = jnp.concatenate([abuf[k, m].astype(F32) for k in range(8)], axis=0)
            wbuf[m, pl.ds(al(s * CHUNK, 16), CHUNK), :] = rows.astype(BF)

    def w_first():
        for m in range(2):
            w_go(s, m, xnb)
        for m in range(2):
            w_go(s, m, sib)

    def w_second():
        w_go(s, 0, zup)
        w_go(s, 1, zdn)
        w_go(s, 1, zup)
        w_go(s, 0, zdn)

    def comm_of(entries):
        plan = []
        for part, (cond, slot, forward, relays) in entries:
            sends = relays + [(cond if forward is None else cond & forward, sib)]
            numbered = []
            for ok, dev in sends:
                numbered.append((ok, dev, len(kv_sent)))
                kv_sent.append((ok, slot, part, dev))
            plan.append((cond, slot, part, numbered))

        def run():
            for cond, slot, part, numbered in plan:

                @pl.when(cond)
                def _(slot=slot, part=part):
                    kv_arrived(slot, part)

                for ok, dev, sem in numbered:

                    @pl.when(ok)
                    def _(slot=slot, part=part, dev=dev, sem=sem):
                        kv_send(slot, part, dev, sem).start()

        return run

    middle = (z == 1) | (z == 2)
    up1 = (up_ok(-1), up_slot(-1, c), None, [(middle, zup)])
    over = (down_ok(0), down_slot(0, c), c == 1, [((x == 1) & (z >= 1), zdn), ((x == 1) & (z == 3), zup)])
    down1 = (down_ok(1), down_slot(1, c), None, [((x == 1) & middle, zdn)])
    up3 = (up_ok(-3), up_slot(-3, c), None, [])
    down3 = (down_ok(3), down_slot(3, c), None, [])
    up2 = (up_ok(-2), up_slot(-2, c), None, [])
    down2 = (down_ok(2), down_slot(2, c), None, [])
    comm_a = comm_of([(0, over), (0, up1), (1, over), (1, up1)])
    comm_b0 = comm_of([(0, down1)])
    comm_b1 = comm_of([(1, down1), (0, up3), (1, up3), (0, down3), (1, down3)])
    comm_c = comm_of([(0, up2), (0, down2), (1, up2), (1, down2)])

    offsets = {2: -1, 3: 0, 4: -1, 5: 0, 6: 1, 7: -3, 8: 3, 9: 1, 10: -3, 11: 3, 12: -2, 13: 2, 14: -2, 15: 2}

    def step(i, carry):
        @pl.when(i == 2)
        def _():
            comm_a()

        @pl.when(i == 4)
        def _():
            comm_b0()
            repack()
            w_first()

        @pl.when(i == 6)
        def _():
            comm_b1()
            w_second()

        @pl.when(i == 12)
        def _():
            comm_c()

        off = 0
        for k, value in offsets.items():
            off = off + jnp.where(i == k, value, 0)
        from_sib = (i == 1) | (i == 4) | (i == 5) | ((i >= 9) & (i <= 11)) | (i >= 14)
        is_down = (i >= 2) & (off >= 0)
        column = jnp.where(is_down, 0, x)
        zz = z + off
        ok = jnp.where(is_down, (x == 1) & (zz <= 3), zz >= 0)
        ok = ok & ((i != 1) | (c == 1)) & ((i != 5) | (c == 0))
        core = jnp.where(from_sib, 1 - c, c)
        slot = column * 8 + (zz + 4) % 4 * 2 + core

        @pl.when(ok & from_sib)
        def _():
            kv_arrived(slot, 0)
            kv_arrived(slot, 1)

        @pl.when(ok)
        def _():
            flash(slot)

        return carry

    lax.fori_loop(0, 16, step, 0)

    for r in range(2):
        att[:, r * HD : (r + 1) * HD] = (acc[r] / lbuf[r, :, 0:1]).astype(BF)

    s_x = (1 - x) * 8 + z * 2 + c
    s_zm = x * 8 + zm * 2 + c
    s_zp = x * 8 + zp * 2 + c
    s_z2 = x * 8 + (z + 2) % 4 * 2 + c
    s_xzm = (1 - x) * 8 + zm * 2 + c
    s_xzp = (1 - x) * 8 + zp * 2 + c
    s_xz2 = (1 - x) * 8 + (z + 2) % 4 * 2 + c

    def w_stage1():
        w_arrived(s_zm, 0)
        w_go(s_zm, 0, zup)
        w_arrived(s_zp, 1)
        w_go(s_zp, 1, zdn)
        for m in range(2):
            w_arrived(s_x, m)
        w_go(s_x, 0, zup)
        w_go(s_x, 1, zdn)
        w_go(s_x, 1, zup)
        w_go(s_x, 0, zdn)
        w_arrived(s_zm, 1)
        w_arrived(s_zp, 0)
        for slot in (s_x, s_zm, s_zp):
            for m in range(2):
                w_go(slot, m, sib)

    def w_stage2():
        for m in range(2):
            w_arrived(s_z2, m)
            w_go(s_z2, m, xnb)
            w_go(s_z2, m, sib)

    def w_stage3():
        for slot in (s_xzm, s_xzp):
            for m in range(2):
                w_arrived(slot, m)
                w_go(slot, m, sib)

    def w_stage4():
        for m in range(2):
            w_arrived(s_xz2, m)
            w_go(s_xz2, m, sib)

    def w_stage5():
        for xx in range(2):
            for zz in range(4):
                for m in range(2):
                    w_arrived(xx * 8 + zz * 2 + 1 - c, m)

    rs_sent = []

    def send(src, dst, recv, dev):
        copy = rcopy(src, dst, rs_s.at[len(rs_sent)], recv, dev)
        copy.start()
        rs_sent.append(copy)

    def rows_of(block):
        return pl.ds(al(block * BLK, 16), BLK)

    cols = (pl.ds(0, HALF), pl.ds(HALF, HALF))
    phase_h = (o, h)

    def rs_start(k, pb, p):
        g = phase_h[p]
        far = rows_of(g * 4 + y2)
        send(pb.at[far, cols[0]], r1.at[k, p, 0], r1_r.at[k, p, 0], yup)
        send(pb.at[far, cols[1]], r1.at[k, p, 1], r1_r.at[k, p, 1], ydn)
        send(pb.at[rows_of(g * 4 + yp), cols[1]], r2.at[k, p, 0, 1], r2_r.at[k, p, 0, 1], yup)
        send(pb.at[rows_of(g * 4 + ym), cols[0]], r2.at[k, p, 1, 0], r2_r.at[k, p, 1, 0], ydn)

    def rs_middle(k, pb, p):
        g = phase_h[p]
        for way, (yy, dev) in enumerate(((yp, yup), (ym, ydn))):
            near = rows_of(g * 4 + yy)
            rcopy(r1.at[k, p, way], r1.at[k, p, way], rs_s.at[0], r1_r.at[k, p, way], dev).wait_recv()
            pb[near, cols[way]] = (
                pb[near, cols[way]].astype(F32) + r1[k, p, way].astype(F32)
            ).astype(BF)
            send(pb.at[near, cols[way]], r2.at[k, p, way, way], r2_r.at[k, p, way, way], dev)

    def rs_end(k, pb, p):
        g = phase_h[p]
        for way in range(2):
            for half in range(2):
                ref = r2.at[k, p, way, half]
                rcopy(ref, ref, rs_s.at[0], r2_r.at[k, p, way, half], yup).wait_recv()
        mine = rows_of(g * 4 + y)
        return jnp.concatenate(
            [
                pb[mine, cols[half]].astype(F32)
                + r2[k, p, 0, half].astype(F32)
                + r2[k, p, 1, half].astype(F32)
                for half in range(2)
            ],
            axis=1,
        )

    def rs_cross(k, pb):
        sx[k] = rs_end(k, pb, 0).astype(BF)
        send(sx.at[k], rx.at[k], rx_r.at[k], xhi)

    def rs_total(k, pb):
        total = rs_end(k, pb, 1)
        rcopy(rx.at[k], rx.at[k], rs_s.at[0], rx_r.at[k], xhi).wait_recv()
        return total + rx[k].astype(F32)

    def normed(values, gain):
        meansq = jnp.mean(values * values, axis=-1, keepdims=True)
        return values * lax.rsqrt(meansq + 1e-06) * gain[...].reshape(1, D)

    ag_sent = []

    def ag_copy(k, ag, block, half, dev, sem):
        ref = ag.at[rows_of(block), cols[half]]
        return rcopy(ref, ref, ag_s.at[sem], ag_r.at[k, block, half], dev)

    def ag_go(k, ag, block, half, dev):
        copy = ag_copy(k, ag, block, half, dev, len(ag_sent))
        copy.start()
        ag_sent.append(copy)

    def ag_arrived(k, ag, block, half):
        ag_copy(k, ag, block, half, xhi, 0).wait_recv()

    def ag_start(k, ag):
        b = h * 4 + y
        ag_go(k, ag, b, 0, xhi)
        ag_go(k, ag, b, 1, xhi)
        ag_go(k, ag, b, 0, yup)
        ag_go(k, ag, b, 1, ydn)
        ag_go(k, ag, b, 1, yup)
        ag_go(k, ag, b, 0, ydn)

    def ag_relay(k, ag, g):
        ag_arrived(k, ag, g * 4 + ym, 0)
        ag_go(k, ag, g * 4 + ym, 0, yup)
        ag_arrived(k, ag, g * 4 + yp, 1)
        ag_go(k, ag, g * 4 + yp, 1, ydn)

    def ag_cross(k, ag):
        b = o * 4 + y
        for half in range(2):
            ag_arrived(k, ag, b, half)
        ag_go(k, ag, b, 0, yup)
        ag_go(k, ag, b, 1, ydn)
        ag_go(k, ag, b, 1, yup)
        ag_go(k, ag, b, 0, ydn)

    def ag_end(k, ag, g):
        ag_arrived(k, ag, g * 4 + ym, 1)
        ag_arrived(k, ag, g * 4 + yp, 0)
        ag_arrived(k, ag, g * 4 + y2, 0)
        ag_arrived(k, ag, g * 4 + y2, 1)

    def group_rows(g):
        return pl.ds(al(g * GROUP, 16), GROUP)

    def project(lhs, weight, g, pb):
        def tile(j, carry):
            at = pl.ds(al(j * 256, 256), 256)
            pb[group_rows(g), at] = jnp.dot(
                lhs[group_rows(g), :], weight[:, at], preferred_element_type=F32
            ).astype(BF)
            return carry

        lax.fori_loop(0, D // 256, tile, 0)

    local_copies[4].wait()
    project(att, owv, o, pb1)
    rs_start(0, pb1, 0)
    project(att, owv, h, pb1)
    rs_middle(0, pb1, 0)
    rs_start(0, pb1, 1)
    rs_cross(0, pb1)
    rs_middle(0, pb1, 1)
    w_stage1()
    local_copies[5].wait()
    total = rs_total(0, pb1)
    mid = hidv[...].astype(F32) + normed(total, g_attn)
    resid[...] = mid
    ag1[rows_of(own_block), :] = normed(mid, g_pre).astype(BF)
    ag_start(0, ag1)
    w_stage2()
    ag_relay(0, ag1, h)
    ag_cross(0, ag1)
    ag_relay(0, ag1, o)
    ag_end(0, ag1, h)
    w_stage3()
    w_stage4()
    w_stage5()

    def ffn(g):
        def tile(j, carry):
            at = pl.ds(al(j * 128, 128), 128)
            both = jnp.concatenate([wbuf[0, :, at], wbuf[1, :, at]], axis=1)
            joint = jnp.dot(ag1[group_rows(g), :], both, preferred_element_type=F32)
            gate = joint[:, :128]
            up = joint[:, 128:]
            inner = 0.7978845608028654 * (gate + 0.044715 * (gate * gate * gate))
            act[group_rows(g), at] = (0.5 * gate * (1.0 + jnp.tanh(inner)) * up).astype(BF)
            return carry

        lax.fori_loop(0, UNITS // 128, tile, 0)

    ffn(h)
    ag_end(0, ag1, o)
    ffn(o)
    local_copies[6].wait()
    project(act, dwv, o, pb2)
    rs_start(1, pb2, 0)
    project(act, dwv, h, pb2)
    rs_middle(1, pb2, 0)
    rs_start(1, pb2, 1)
    rs_cross(1, pb2)
    rs_middle(1, pb2, 1)
    total = rs_total(1, pb2)
    last = resid[...] + normed(total, g_post)
    ag2[rows_of(own_block), :] = normed(last, g_next).astype(BF)
    ag_start(1, ag2)
    ag_relay(1, ag2, h)
    ag_cross(1, ag2)
    ag_end(1, ag2, h)
    ag_relay(1, ag2, o)
    local_copies[7].wait()

    def next_qkv(g):
        def tile(j, carry):
            at = pl.ds(al(j * 256, 256), 256)
            out[group_rows(g), at] = jnp.dot(
                ag2[group_rows(g), :], nwv[:, at], preferred_element_type=F32
            ).astype(BF)
            return carry

        lax.fori_loop(0, QKV // 256, tile, 0)

    next_qkv(h)
    ag_end(1, ag2, o)
    next_qkv(o)

    for sem, (cond, slot, part, dev) in enumerate(kv_sent):

        @pl.when(cond)
        def _(slot=slot, part=part, dev=dev, sem=sem):
            kv_send(slot, part, dev, sem).wait_send()

    for k in range(1, 8):
        a_send(k).wait_send()
    for sem, (slot, m, dev) in enumerate(w_sent):
        w_copy(slot, m, dev, sem).wait_send()
    for copy in rs_sent + ag_sent:
        copy.wait_send()


def local(hid, joined, lengths, ow, gu, dw, nw, g_attn, g_pre, g_post, g_next):
    hbm = pl.BlockSpec(memory_space=pl.ANY)
    vmem = pl.BlockSpec(memory_space=pltpu.VMEM)
    smem = pl.BlockSpec(memory_space=pltpu.SMEM)
    V = pltpu.VMEM
    DMA = pltpu.SemaphoreType.DMA
    scratch = [
        V((2, ROWS, HD), BF),
        V((16, 2, ROWS, HD), BF),
        V(ow.shape, BF),
        V(dw.shape, BF),
        V(nw.shape, BF),
        V((BLK, D), BF),
        V((PIECE, 2, gu.shape[2]), F32),
        V((8, 2, PIECE, UNITS), BF),
        V((8, 2, PIECE, UNITS), BF),
        V((2, D, UNITS), BF),
        V((2, ROWS, 1), F32),
        V((2, ROWS, 1), F32),
        V((2, ROWS, HD), F32),
        V((ROWS, 2 * HD), BF),
        V((ROWS, D), BF),
        V((ROWS, D), BF),
        V((2, 2, 2, BLK, HALF), BF),
        V((2, 2, 2, 2, BLK, HALF), BF),
        V((2, BLK, D), BF),
        V((2, BLK, D), BF),
        V((ROWS, D), BF),
        V((ROWS, D), BF),
        V((ROWS, UNITS), BF),
        V((BLK, D), F32),
        DMA((9,)),
        DMA((36,)),
        DMA((16, 2)),
        DMA((8,)),
        DMA((8,)),
        DMA((48,)),
        DMA((16, 2)),
        DMA((2, 2, 2)),
        DMA((2, 2, 2, 2)),
        DMA((2,)),
        DMA((32,)),
        DMA((40,)),
        DMA((2, 8, 2)),
    ]
    return pl.pallas_call(
        kernel,
        out_shape=jax.ShapeDtypeStruct((ROWS, QKV), BF),
        in_specs=[smem, hbm, hbm, hbm, hbm, hbm, hbm, vmem, vmem, vmem, vmem],
        out_specs=vmem,
        scratch_shapes=scratch,
        compiler_params=pltpu.CompilerParams(
            collective_id=0, has_side_effects=True, vmem_limit_bytes=67043328
        ),
    )(
        lengths, hid, joined, ow, gu.transpose(1, 0, 2), dw, nw,
        g_attn, g_pre, g_post, g_next,
    )


def solution(mesh):
    in_specs = (
        P("seq", None),
        P("seq", "tp"),
        P(),
        P("tp", None),
        P(None, ("seq", "tp"), None),
        P("tp", None),
        P(None, "tp"),
        P(),
        P(),
        P(),
        P(),
    )
    return jax.shard_map(
        local, mesh=mesh, in_specs=in_specs, out_specs=P("seq", "tp"), check_vma=False
    )
```

```python
import jax
import jax.numpy as jnp
from jax import lax
from jax.experimental import pallas as pl
from jax.experimental.pallas import tpu as pltpu
from jax.sharding import PartitionSpec as P

MESH = pl.DeviceIdType.MESH
BF = jnp.bfloat16
F32 = jnp.float32
D = 3584
PART_A = 1536
PART_B = D - PART_A
ROWS = 384
HD = 256
UNITS = 896
PIECE = 28
CHUNK = 224
BLK = 48
GROUP = 192
QKV = 1024
NEG = -1e30


def al(value, to):
    return pl.multiple_of(value, to)


def kernel(
    lens, hid, joined, ow, gu, dw, nw, g_attn, g_pre, g_post, g_next,
    out,
    qbuf, kvbuf, owv, dwv, nwv, hidv, guv, gub, abuf, wbuf,
    mbuf, lbuf, acc, att, pb1, pb2, r1b, r2b, r1a, r2a, rxa, rx, sx, ag1, ag2, act, resid,
    lsem, kv_s, kv_r, a_s, a_r, w_s, w_r, r1_r, r2_r, rxa_r, rx_r, rs_s, ag_s, ag_r,
):
    s = lax.axis_index("seq")
    t = lax.axis_index("tp")
    x = s // 8
    z = (s // 2) % 4
    c = s % 2
    y = t // 2
    h = t % 2
    o = 1 - h

    def dev_seq(xx, zz, cc):
        return (xx * 8 + zz * 2 + cc, t)

    def dev_tp(yy, hh):
        return (s, yy * 2 + hh)

    zp, zm = (z + 1) % 4, (z + 3) % 4
    yp, ym, y2 = (y + 1) % 4, (y + 3) % 4, (y + 2) % 4
    sib = dev_seq(x, z, 1 - c)
    xnb = dev_seq(1 - x, z, c)
    zup = dev_seq(x, zp, c)
    zdn = dev_seq(x, zm, c)
    yup = dev_tp(yp, h)
    ydn = dev_tp(ym, h)
    xhi = dev_tp(y, o)

    barrier = pltpu.get_barrier_semaphore()
    tp_peers = [(s, (t + k) % 8) for k in range(1, 8)]
    for peer in [sib, xnb, zup, zdn] + tp_peers:
        pl.semaphore_signal(barrier, inc=1, device_id=peer, device_id_type=MESH)

    own_block = h * 4 + y
    loads = [
        (joined.at[:, pl.ds(512, 256)], kvbuf.at[s, 0]),
        (joined.at[:, pl.ds(0, 256)], qbuf.at[0]),
        (joined.at[:, pl.ds(256, 256)], qbuf.at[1]),
        (gu, guv),
        (ow, owv),
        (hid.at[pl.ds(al(own_block * BLK, 16), BLK), :], hidv),
        (dw, dwv),
        (nw, nwv),
        (joined.at[:, pl.ds(768, 256)], kvbuf.at[s, 1]),
    ]
    local_copies = [
        pltpu.make_async_copy(src, dst, lsem.at[i]) for i, (src, dst) in enumerate(loads)
    ]
    for copy in local_copies:
        copy.start()

    def rcopy(src, dst, send, recv, dev):
        return pltpu.make_async_remote_copy(
            src_ref=src,
            dst_ref=dst,
            send_sem=send,
            recv_sem=recv,
            device_id=dev,
            device_id_type=MESH,
        )

    pl.semaphore_wait(barrier, 11)

    def kv_send(slot, part, dev, sem):
        ref = kvbuf.at[slot, part]
        return rcopy(ref, ref, kv_s.at[sem], kv_r.at[slot, part], dev)

    def kv_arrived(slot, part):
        kv_send(slot, part, sib, 0).wait_recv()

    kv_sent = []
    for part in range(2):
        local_copies[(0, 8)[part]].wait()
        for ok, dev in ((z < 3, zup), (x == 0, xnb), (z == 0, zdn), (c == 0, sib)):
            sem = len(kv_sent)
            kv_sent.append((ok, s, part, dev))

            @pl.when(ok)
            def _(part=part, dev=dev, sem=sem):
                kv_send(s, part, dev, sem).start()

    local_copies[3].wait()
    for k in range(8):
        for m in range(2):
            gub[k, m] = guv[:, m, k * UNITS : (k + 1) * UNITS].astype(BF)

    def a_send(k):
        peer = (t + k) % 8
        return rcopy(gub.at[peer], abuf.at[t], a_s.at[k], a_r.at[k], (s, peer))

    for k in range(1, 8):
        a_send(k).start()

    local_copies[1].wait()
    local_copies[2].wait()
    mbuf[...] = jnp.full(mbuf.shape, NEG, F32)
    lbuf[...] = jnp.zeros(lbuf.shape, F32)
    acc[...] = jnp.zeros(acc.shape, F32)

    end0 = lens[0]
    end1 = end0 + lens[1]
    end2 = end1 + lens[2]

    def flash(slot):
        place = s * ROWS + lax.broadcasted_iota(jnp.int32, (ROWS, 1), 0)
        low = jnp.where(
            place >= end2,
            end2,
            jnp.where(place >= end1, end1, jnp.where(place >= end0, end0, 0)),
        )
        other = slot * ROWS + lax.broadcasted_iota(jnp.int32, (ROWS, ROWS), 1)
        allowed = (other >= low) & (other <= place)

        def head(r, carry):
            scores = lax.dot_general(
                qbuf[r],
                kvbuf[slot, 0],
                (((1,), (1,)), ((), ())),
                preferred_element_type=F32,
            ) * (HD ** -0.5)
            scores = jnp.where(allowed, scores, NEG)
            before = mbuf[r]
            peak = jnp.maximum(before, jnp.max(scores, axis=-1, keepdims=True))
            weights = jnp.exp(scores - peak)
            fade = jnp.exp(before - peak)
            lbuf[r] = lbuf[r] * fade + jnp.sum(weights, axis=-1, keepdims=True)
            mbuf[r] = peak
            acc[r] = acc[r] * fade + jnp.dot(
                weights.astype(BF), kvbuf[slot, 1], preferred_element_type=F32
            )
            return carry

        lax.fori_loop(0, 2, head, 0)

    def up_ok(off):
        return z + off >= 0

    def down_ok(off):
        return (x == 1) & (z + off <= 3)

    def up_slot(off, core):
        return x * 8 + (z + off + 4) % 4 * 2 + core

    def down_slot(off, core):
        return (z + off) % 4 * 2 + core

    def w_ref(slot, m):
        return wbuf.at[m, pl.ds(al(slot * CHUNK, 16), CHUNK), :]

    w_sent = []

    def w_copy(slot, m, dev, sem):
        return rcopy(w_ref(slot, m), w_ref(slot, m), w_s.at[sem], w_r.at[slot, m], dev)

    def w_go(slot, m, dev):
        w_copy(slot, m, dev, len(w_sent)).start()
        w_sent.append((slot, m, dev))

    def w_arrived(slot, m):
        w_copy(slot, m, sib, 0).wait_recv()

    def repack():
        for k in range(1, 8):
            peer = (t + 8 - k) % 8
            rcopy(gub.at[0], abuf.at[peer], a_s.at[k], a_r.at[k], (s, peer)).wait_recv()
        abuf[t] = gub[t]
        for m in range(2):
            rows = jnp.concatenate([abuf[k, m].astype(F32) for k in range(8)], axis=0)
            wbuf[m, pl.ds(al(s * CHUNK, 16), CHUNK), :] = rows.astype(BF)

    def w_first():
        for m in range(2):
            w_go(s, m, xnb)
        for m in range(2):
            w_go(s, m, sib)

    def w_second():
        w_go(s, 0, zup)
        w_go(s, 1, zdn)
        w_go(s, 1, zup)
        w_go(s, 0, zdn)

    def comm_of(entries):
        plan = []
        for part, (cond, slot, forward, relays) in entries:
            sends = relays + [(cond if forward is None else cond & forward, sib)]
            numbered = []
            for ok, dev in sends:
                numbered.append((ok, dev, len(kv_sent)))
                kv_sent.append((ok, slot, part, dev))
            plan.append((cond, slot, part, numbered))

        def run():
            for cond, slot, part, numbered in plan:

                @pl.when(cond)
                def _(slot=slot, part=part):
                    kv_arrived(slot, part)

                for ok, dev, sem in numbered:

                    @pl.when(ok)
                    def _(slot=slot, part=part, dev=dev, sem=sem):
                        kv_send(slot, part, dev, sem).start()

        return run

    middle = (z == 1) | (z == 2)
    up1 = (up_ok(-1), up_slot(-1, c), None, [(middle, zup)])
    over = (down_ok(0), down_slot(0, c), c == 1, [((x == 1) & (z >= 1), zdn), ((x == 1) & (z == 3), zup)])
    down1 = (down_ok(1), down_slot(1, c), None, [((x == 1) & middle, zdn)])
    up3 = (up_ok(-3), up_slot(-3, c), None, [])
    down3 = (down_ok(3), down_slot(3, c), None, [])
    up2 = (up_ok(-2), up_slot(-2, c), None, [])
    down2 = (down_ok(2), down_slot(2, c), None, [])
    comm_a = comm_of([(0, over), (0, up1), (1, over), (1, up1)])
    comm_b0 = comm_of([(0, down1)])
    comm_b1 = comm_of([(1, down1), (0, up3), (1, up3), (0, down3), (1, down3)])
    comm_c = comm_of([(0, up2), (0, down2), (1, up2), (1, down2)])

    offsets = {2: -1, 3: 0, 4: -1, 5: 0, 6: 1, 7: -3, 8: 3, 9: 1, 10: -3, 11: 3, 12: -2, 13: 2, 14: -2, 15: 2}

    def step(i, carry):
        @pl.when(i == 2)
        def _():
            comm_a()

        @pl.when(i == 4)
        def _():
            comm_b0()
            repack()
            w_first()

        @pl.when(i == 6)
        def _():
            comm_b1()
            w_second()

        @pl.when(i == 12)
        def _():
            comm_c()

        off = 0
        for k, value in offsets.items():
            off = off + jnp.where(i == k, value, 0)
        from_sib = (i == 1) | (i == 4) | (i == 5) | ((i >= 9) & (i <= 11)) | (i >= 14)
        is_down = (i >= 2) & (off >= 0)
        column = jnp.where(is_down, 0, x)
        zz = z + off
        ok = jnp.where(is_down, (x == 1) & (zz <= 3), zz >= 0)
        ok = ok & ((i != 1) | (c == 1)) & ((i != 5) | (c == 0))
        core = jnp.where(from_sib, 1 - c, c)
        slot = column * 8 + (zz + 4) % 4 * 2 + core

        @pl.when(ok & from_sib)
        def _():
            kv_arrived(slot, 0)
            kv_arrived(slot, 1)

        @pl.when(ok)
        def _():
            flash(slot)

        return carry

    lax.fori_loop(0, 16, step, 0)

    for r in range(2):
        att[:, r * HD : (r + 1) * HD] = (acc[r] / lbuf[r, :, 0:1]).astype(BF)

    s_x = (1 - x) * 8 + z * 2 + c
    s_zm = x * 8 + zm * 2 + c
    s_zp = x * 8 + zp * 2 + c
    s_z2 = x * 8 + (z + 2) % 4 * 2 + c
    s_xzm = (1 - x) * 8 + zm * 2 + c
    s_xzp = (1 - x) * 8 + zp * 2 + c
    s_xz2 = (1 - x) * 8 + (z + 2) % 4 * 2 + c

    def w_over():
        for m in range(2):
            w_arrived(s_x, m)
        w_go(s_x, 0, zup)
        w_go(s_x, 1, zdn)
        w_go(s_x, 1, zup)
        w_go(s_x, 0, zdn)
        for m in range(2):
            w_go(s_x, m, sib)

    def w_relay():
        w_arrived(s_zm, 0)
        w_go(s_zm, 0, zup)
        w_arrived(s_zp, 1)
        w_go(s_zp, 1, zdn)
        w_arrived(s_zm, 1)
        w_arrived(s_zp, 0)
        for slot in (s_zm, s_zp):
            for m in range(2):
                w_go(slot, m, sib)

    def w_relay_over():
        w_arrived(s_xzm, 0)
        w_go(s_xzm, 0, zup)
        w_arrived(s_xzp, 1)
        w_go(s_xzp, 1, zdn)
        w_arrived(s_xzm, 1)
        w_arrived(s_xzp, 0)
        for m in range(2):
            w_arrived(s_z2, m)
        for slot in (s_xzm, s_xzp, s_z2):
            for m in range(2):
                w_go(slot, m, sib)

    def w_end():
        for m in range(2):
            w_arrived(s_xz2, m)
            w_go(s_xz2, m, sib)
        for xx in range(2):
            for zz in range(4):
                for m in range(2):
                    w_arrived(xx * 8 + zz * 2 + 1 - c, m)

    rs_sent = []

    def send(src, dst, recv, dev):
        copy = rcopy(src, dst, rs_s.at[len(rs_sent)], recv, dev)
        copy.start()
        rs_sent.append(copy)

    def rows_of(block):
        return pl.ds(al(block * BLK, 16), BLK)

    cols = (
        (pl.ds(0, PART_A // 2), pl.ds(PART_A // 2, PART_A // 2)),
        (pl.ds(PART_A, PART_B // 2), pl.ds(PART_A + PART_B // 2, PART_B // 2)),
    )
    first = pl.ds(0, PART_A)
    lanes = ((1, o), (1, h), (0, h))

    def r1_at(k, lane, way):
        return r1b.at[k, lane, way] if lane < 2 else r1a.at[k, way]

    def r2_at(k, lane, way, half):
        return r2b.at[k, lane, way, half] if lane < 2 else r2a.at[k, way, half]

    def arrived(ref, recv):
        rcopy(ref, ref, rs_s.at[0], recv, xhi).wait_recv()

    def rs_far(k, pb, lane):
        part, g = lanes[lane]
        far = rows_of(g * 4 + y2)
        send(pb.at[far, cols[part][0]], r1_at(k, lane, 0), r1_r.at[k, lane, 0], yup)
        send(pb.at[far, cols[part][1]], r1_at(k, lane, 1), r1_r.at[k, lane, 1], ydn)

    def rs_near(k, pb, lane):
        part, g = lanes[lane]
        send(pb.at[rows_of(g * 4 + yp), cols[part][1]], r2_at(k, lane, 0, 1), r2_r.at[k, lane, 0, 1], yup)
        send(pb.at[rows_of(g * 4 + ym), cols[part][0]], r2_at(k, lane, 1, 0), r2_r.at[k, lane, 1, 0], ydn)

    def rs_middle(k, pb, lane):
        part, g = lanes[lane]
        for way, (yy, dev) in enumerate(((yp, yup), (ym, ydn))):
            near = rows_of(g * 4 + yy)
            ref = r1_at(k, lane, way)
            arrived(ref, r1_r.at[k, lane, way])
            pb[near, cols[part][way]] = (
                pb[near, cols[part][way]].astype(F32) + ref[...].astype(F32)
            ).astype(BF)
            send(pb.at[near, cols[part][way]], r2_at(k, lane, way, way), r2_r.at[k, lane, way, way], dev)

    def rs_end(k, pb, lane):
        part, g = lanes[lane]
        for way in range(2):
            for half in range(2):
                arrived(r2_at(k, lane, way, half), r2_r.at[k, lane, way, half])
        mine = rows_of(g * 4 + y)
        return jnp.concatenate(
            [
                pb[mine, cols[part][half]].astype(F32)
                + r2_at(k, lane, 0, half)[...].astype(F32)
                + r2_at(k, lane, 1, half)[...].astype(F32)
                for half in range(2)
            ],
            axis=1,
        )

    def rs_over(k, pb):
        for yy in (y2, yp, ym, y):
            send(pb.at[rows_of(o * 4 + yy), first], rxa.at[k, yy], rxa_r.at[k, yy], xhi)

    def rs_add(k, pb, yy):
        arrived(rxa.at[k, yy], rxa_r.at[k, yy])
        at = rows_of(h * 4 + yy)
        pb[at, first] = (pb[at, first].astype(F32) + rxa[k, yy].astype(F32)).astype(BF)

    def tp_sum(k, lhs, weight, pb, pump0, pump1):
        project(lhs, weight, o, pb)
        rs_over(k, pb)
        rs_far(k, pb, 0)
        rs_near(k, pb, 0)
        project(lhs, weight, h, pb)
        rs_middle(k, pb, 0)
        pump0()
        rs_add(k, pb, y2)
        rs_far(k, pb, 2)
        rs_far(k, pb, 1)
        rs_near(k, pb, 1)
        sx[k] = rs_end(k, pb, 0).astype(BF)
        send(sx.at[k], rx.at[k], rx_r.at[k], xhi)
        rs_middle(k, pb, 1)
        rs_add(k, pb, yp)
        rs_add(k, pb, ym)
        rs_near(k, pb, 2)
        rs_middle(k, pb, 2)
        pump1()
        part_b = rs_end(k, pb, 1)
        arrived(rxa.at[k, y], rxa_r.at[k, y])
        part_a = rs_end(k, pb, 2) + rxa[k, y].astype(F32)
        arrived(rx.at[k], rx_r.at[k])
        return jnp.concatenate([part_a, part_b + rx[k].astype(F32)], axis=1)

    def normed(values, gain):
        meansq = jnp.mean(values * values, axis=-1, keepdims=True)
        return values * lax.rsqrt(meansq + 1e-06) * gain[...].reshape(1, D)

    ag_sent = []

    def ag_copy(k, ag, block, part, half, dev, sem):
        ref = ag.at[rows_of(block), cols[part][half]]
        return rcopy(ref, ref, ag_s.at[sem], ag_r.at[k, block, part * 2 + half], dev)

    def ag_go(k, ag, block, part, half, dev):
        copy = ag_copy(k, ag, block, part, half, dev, len(ag_sent))
        copy.start()
        ag_sent.append(copy)

    def ag_arrived(k, ag, block, part, half):
        ag_copy(k, ag, block, part, half, xhi, 0).wait_recv()

    def ag_both(k, ag, block, part):
        ag_go(k, ag, block, part, 0, yup)
        ag_go(k, ag, block, part, 1, ydn)
        ag_go(k, ag, block, part, 1, yup)
        ag_go(k, ag, block, part, 0, ydn)

    def ag_relay(k, ag, g, part):
        ag_arrived(k, ag, g * 4 + ym, part, 0)
        ag_go(k, ag, g * 4 + ym, part, 0, yup)
        ag_arrived(k, ag, g * 4 + yp, part, 1)
        ag_go(k, ag, g * 4 + yp, part, 1, ydn)

    def ag_rest(k, ag, g, part):
        ag_arrived(k, ag, g * 4 + ym, part, 1)
        ag_arrived(k, ag, g * 4 + yp, part, 0)

    def ag_far(k, ag, g, part):
        ag_arrived(k, ag, g * 4 + y2, part, 0)
        ag_arrived(k, ag, g * 4 + y2, part, 1)

    def tp_gather(k, ag, pump0, pump1):
        own = h * 4 + y
        for half in range(2):
            ag_go(k, ag, own, 1, half, xhi)
        ag_both(k, ag, own, 0)
        for half in range(2):
            ag_go(k, ag, own, 0, half, xhi)
        ag_both(k, ag, own, 1)
        ag_relay(k, ag, h, 0)
        ag_rest(k, ag, h, 0)
        for yy in (ym, yp):
            for half in range(2):
                ag_go(k, ag, h * 4 + yy, 0, half, xhi)
        pump0()
        for half in range(2):
            ag_arrived(k, ag, o * 4 + y, 1, half)
        ag_relay(k, ag, h, 1)
        ag_both(k, ag, o * 4 + y, 1)
        ag_far(k, ag, h, 0)
        for half in range(2):
            ag_go(k, ag, h * 4 + y2, 0, half, xhi)
        pump1()
        ag_relay(k, ag, o, 1)
        ag_rest(k, ag, h, 1)
        ag_far(k, ag, h, 1)

    def tp_gathered(k, ag):
        ag_rest(k, ag, o, 1)
        ag_far(k, ag, o, 1)
        for yy in range(4):
            for half in range(2):
                ag_arrived(k, ag, o * 4 + yy, 0, half)

    def group_rows(g):
        return pl.ds(al(g * GROUP, 16), GROUP)

    def project(lhs, weight, g, pb):
        def tile(j, carry):
            at = pl.ds(al(j * 256, 256), 256)
            pb[group_rows(g), at] = jnp.dot(
                lhs[group_rows(g), :], weight[:, at], preferred_element_type=F32
            ).astype(BF)
            return carry

        lax.fori_loop(0, D // 256, tile, 0)

    def nothing():
        pass

    local_copies[4].wait()
    w_over()
    total = tp_sum(0, att, owv, pb1, nothing, w_relay)
    local_copies[5].wait()
    mid = hidv[...].astype(F32) + normed(total, g_attn)
    resid[...] = mid
    ag1[rows_of(own_block), :] = normed(mid, g_pre).astype(BF)
    tp_gather(0, ag1, nothing, w_relay_over)
    w_end()

    def ffn(g):
        def tile(j, carry):
            at = pl.ds(al(j * 128, 128), 128)
            both = jnp.concatenate([wbuf[0, :, at], wbuf[1, :, at]], axis=1)
            joint = jnp.dot(ag1[group_rows(g), :], both, preferred_element_type=F32)
            gate = joint[:, :128]
            up = joint[:, 128:]
            inner = 0.7978845608028654 * (gate + 0.044715 * (gate * gate * gate))
            act[group_rows(g), at] = (0.5 * gate * (1.0 + jnp.tanh(inner)) * up).astype(BF)
            return carry

        lax.fori_loop(0, UNITS // 128, tile, 0)

    ffn(h)
    tp_gathered(0, ag1)
    ffn(o)
    local_copies[6].wait()
    total = tp_sum(1, act, dwv, pb2, nothing, nothing)
    last = resid[...] + normed(total, g_post)
    ag2[rows_of(own_block), :] = normed(last, g_next).astype(BF)
    tp_gather(1, ag2, nothing, nothing)
    local_copies[7].wait()

    def next_qkv(g):
        def tile(j, carry):
            at = pl.ds(al(j * 256, 256), 256)
            out[group_rows(g), at] = jnp.dot(
                ag2[group_rows(g), :], nwv[:, at], preferred_element_type=F32
            ).astype(BF)
            return carry

        lax.fori_loop(0, QKV // 256, tile, 0)

    next_qkv(h)
    tp_gathered(1, ag2)
    next_qkv(o)

    for sem, (cond, slot, part, dev) in enumerate(kv_sent):

        @pl.when(cond)
        def _(slot=slot, part=part, dev=dev, sem=sem):
            kv_send(slot, part, dev, sem).wait_send()

    for k in range(1, 8):
        a_send(k).wait_send()
    for sem, (slot, m, dev) in enumerate(w_sent):
        w_copy(slot, m, dev, sem).wait_send()
    for copy in rs_sent + ag_sent:
        copy.wait_send()


def local(hid, joined, lengths, ow, gu, dw, nw, g_attn, g_pre, g_post, g_next):
    hbm = pl.BlockSpec(memory_space=pl.ANY)
    vmem = pl.BlockSpec(memory_space=pltpu.VMEM)
    smem = pl.BlockSpec(memory_space=pltpu.SMEM)
    V = pltpu.VMEM
    DMA = pltpu.SemaphoreType.DMA
    scratch = [
        V((2, ROWS, HD), BF),
        V((16, 2, ROWS, HD), BF),
        V(ow.shape, BF),
        V(dw.shape, BF),
        V(nw.shape, BF),
        V((BLK, D), BF),
        V((PIECE, 2, gu.shape[2]), F32),
        V((8, 2, PIECE, UNITS), BF),
        V((8, 2, PIECE, UNITS), BF),
        V((2, D, UNITS), BF),
        V((2, ROWS, 1), F32),
        V((2, ROWS, 1), F32),
        V((2, ROWS, HD), F32),
        V((ROWS, 2 * HD), BF),
        V((ROWS, D), BF),
        V((ROWS, D), BF),
        V((2, 2, 2, BLK, PART_B // 2), BF),
        V((2, 2, 2, 2, BLK, PART_B // 2), BF),
        V((2, 2, BLK, PART_A // 2), BF),
        V((2, 2, 2, BLK, PART_A // 2), BF),
        V((2, 4, BLK, PART_A), BF),
        V((2, BLK, PART_B), BF),
        V((2, BLK, PART_B), BF),
        V((ROWS, D), BF),
        V((ROWS, D), BF),
        V((ROWS, UNITS), BF),
        V((BLK, D), F32),
        DMA((9,)),
        DMA((36,)),
        DMA((16, 2)),
        DMA((8,)),
        DMA((8,)),
        DMA((48,)),
        DMA((16, 2)),
        DMA((2, 3, 2)),
        DMA((2, 3, 2, 2)),
        DMA((2, 4)),
        DMA((2,)),
        DMA((48,)),
        DMA((64,)),
        DMA((2, 8, 4)),
    ]
    return pl.pallas_call(
        kernel,
        out_shape=jax.ShapeDtypeStruct((ROWS, QKV), BF),
        in_specs=[smem, hbm, hbm, hbm, hbm, hbm, hbm, vmem, vmem, vmem, vmem],
        out_specs=vmem,
        scratch_shapes=scratch,
        compiler_params=pltpu.CompilerParams(
            collective_id=0, has_side_effects=True, vmem_limit_bytes=67043328
        ),
    )(
        lengths, hid, joined, ow, gu.transpose(1, 0, 2), dw, nw,
        g_attn, g_pre, g_post, g_next,
    )


def solution(mesh):
    in_specs = (
        P("seq", None),
        P("seq", "tp"),
        P(),
        P("tp", None),
        P(None, ("seq", "tp"), None),
        P("tp", None),
        P(None, "tp"),
        P(),
        P(),
        P(),
        P(),
    )
    return jax.shard_map(
        local, mesh=mesh, in_specs=in_specs, out_specs=P("seq", "tp"), check_vma=False
    )
```

```python
import jax
import jax.numpy as jnp
from jax import lax
from jax.experimental import pallas as pl
from jax.experimental.pallas import tpu as pltpu
from jax.sharding import PartitionSpec as P

MESH = pl.DeviceIdType.MESH
BF = jnp.bfloat16
F32 = jnp.float32
D = 3584
PART_A = 1536
PART_B = D - PART_A
ROWS = 384
HD = 256
UNITS = 896
PIECE = 28
CHUNK = 224
BLK = 48
GROUP = 192
QKV = 1024
NEG = -1e30


def al(value, to):
    return pl.multiple_of(value, to)


def kernel(
    lens, hid, joined, ow, gu, dw, nw, g_attn, g_pre, g_post, g_next,
    out,
    qbuf, kvbuf, owv, dwv, nwv, hidv, guv, gub, abuf, wbuf,
    lowbuf, mbuf, lbuf, acc, att, pb1, pb2, r1b, r2b, r1a, r2a, rxa, rx, sx, ag1, ag2, act, resid,
    lsem, kv_s, kv_r, a_s, a_r, w_s, w_r, r1_r, r2_r, rxa_r, rx_r, rs_s, ag_s, ag_r,
):
    s = lax.axis_index("seq")
    t = lax.axis_index("tp")
    x = s // 8
    z = (s // 2) % 4
    c = s % 2
    y = t // 2
    h = t % 2
    o = 1 - h

    def dev_seq(xx, zz, cc):
        return (xx * 8 + zz * 2 + cc, t)

    def dev_tp(yy, hh):
        return (s, yy * 2 + hh)

    zp, zm = (z + 1) % 4, (z + 3) % 4
    yp, ym, y2 = (y + 1) % 4, (y + 3) % 4, (y + 2) % 4
    sib = dev_seq(x, z, 1 - c)
    xnb = dev_seq(1 - x, z, c)
    zup = dev_seq(x, zp, c)
    zdn = dev_seq(x, zm, c)
    yup = dev_tp(yp, h)
    ydn = dev_tp(ym, h)
    xhi = dev_tp(y, o)

    barrier = pltpu.get_barrier_semaphore()
    tp_peers = [(s, (t + k) % 8) for k in range(1, 8)]
    for peer in [sib, xnb, zup, zdn] + tp_peers:
        pl.semaphore_signal(barrier, inc=1, device_id=peer, device_id_type=MESH)

    own_block = h * 4 + y
    loads = [
        (joined.at[:, pl.ds(512, 256)], kvbuf.at[s, 0]),
        (joined.at[:, pl.ds(0, 256)], qbuf.at[0]),
        (joined.at[:, pl.ds(256, 256)], qbuf.at[1]),
        (gu.at[:, 0, :], guv.at[0]),
        (ow, owv),
        (hid.at[pl.ds(al(own_block * BLK, 16), BLK), :], hidv),
        (dw, dwv),
        (nw, nwv),
        (joined.at[:, pl.ds(768, 256)], kvbuf.at[s, 1]),
        (gu.at[:, 1, :], guv.at[1]),
    ]
    local_copies = [
        pltpu.make_async_copy(src, dst, lsem.at[i]) for i, (src, dst) in enumerate(loads)
    ]
    for i in (0, 8, 3, 9, 1, 2):
        local_copies[i].start()

    def rcopy(src, dst, send, recv, dev):
        return pltpu.make_async_remote_copy(
            src_ref=src,
            dst_ref=dst,
            send_sem=send,
            recv_sem=recv,
            device_id=dev,
            device_id_type=MESH,
        )

    pl.semaphore_wait(barrier, 11)

    def kv_send(slot, part, dev, sem):
        ref = kvbuf.at[slot, part]
        return rcopy(ref, ref, kv_s.at[sem], kv_r.at[slot, part], dev)

    def kv_arrived(slot, part):
        kv_send(slot, part, sib, 0).wait_recv()

    kv_sent = []
    for part in range(2):
        local_copies[(0, 8)[part]].wait()
        outs = [(z < 3, zup), (x == 0, xnb), (z == 0, zdn), (c == 0, sib)]
        if part == 1:
            outs.append(((x == 0) & (z >= 2), zdn))
        for ok, dev in outs:
            sem = len(kv_sent)
            kv_sent.append((ok, s, part, dev))

            @pl.when(ok)
            def _(part=part, dev=dev, sem=sem):
                kv_send(s, part, dev, sem).start()

    local_copies[3].wait()
    local_copies[9].wait()
    for i in (4, 5, 6, 7):
        local_copies[i].start()
    for k in range(8):
        for m in range(2):
            gub[k, m] = guv[m, :, k * UNITS : (k + 1) * UNITS].astype(BF)

    def a_send(k):
        peer = (t + k) % 8
        return rcopy(gub.at[peer], abuf.at[t], a_s.at[k], a_r.at[k], (s, peer))

    for k in range(1, 8):
        a_send(k).start()

    local_copies[1].wait()
    local_copies[2].wait()
    end0 = lens[0]
    end1 = end0 + lens[1]
    end2 = end1 + lens[2]

    place = s * ROWS + lax.broadcasted_iota(jnp.int32, (ROWS, 1), 0)
    low = jnp.where(
        place >= end2,
        end2,
        jnp.where(place >= end1, end1, jnp.where(place >= end0, end0, 0)),
    )
    lowbuf[...] = low

    def flash(slot, own):
        other = slot * ROWS + lax.broadcasted_iota(jnp.int32, (ROWS, ROWS), 1)
        allowed = other >= lowbuf[...]
        if own:
            allowed = allowed & (other <= place)
        for r in range(2):
            scores = lax.dot_general(
                qbuf[r],
                kvbuf[slot, 0],
                (((1,), (1,)), ((), ())),
                preferred_element_type=F32,
            ) * (HD ** -0.5 * 1.4426950408889634)
            scores = jnp.where(allowed, scores, NEG)
            peak = jnp.max(scores, axis=-1, keepdims=True)
            if not own:
                before = mbuf[r]
                peak = jnp.maximum(before, peak)
            weights = jnp.exp2(scores - peak)
            total = jnp.sum(weights, axis=-1, keepdims=True)
            blend = jnp.dot(weights.astype(BF), kvbuf[slot, 1], preferred_element_type=F32)
            if not own:
                fade = jnp.exp2(before - peak)
                total = total + lbuf[r] * fade
                blend = blend + acc[r] * fade
            lbuf[r] = total
            mbuf[r] = peak
            acc[r] = blend

    def up_ok(off):
        return z + off >= 0

    def down_ok(off):
        return (x == 1) & (z + off <= 3)

    def up_slot(off, core):
        return x * 8 + (z + off + 4) % 4 * 2 + core

    def down_slot(off, core):
        return (z + off) % 4 * 2 + core

    def w_ref(slot, m):
        return wbuf.at[m, pl.ds(al(slot * CHUNK, 16), CHUNK), :]

    w_sent = []

    def w_copy(slot, m, dev, sem):
        return rcopy(w_ref(slot, m), w_ref(slot, m), w_s.at[sem], w_r.at[slot, m], dev)

    def w_go(slot, m, dev):
        w_copy(slot, m, dev, len(w_sent)).start()
        w_sent.append((slot, m, dev))

    def w_arrived(slot, m):
        w_copy(slot, m, sib, 0).wait_recv()

    def repack():
        for k in range(1, 8):
            peer = (t + 8 - k) % 8
            rcopy(gub.at[0], abuf.at[peer], a_s.at[k], a_r.at[k], (s, peer)).wait_recv()
        abuf[t] = gub[t]
        for m in range(2):
            rows = jnp.concatenate([abuf[k, m].astype(F32) for k in range(8)], axis=0)
            wbuf[m, pl.ds(al(s * CHUNK, 16), CHUNK), :] = rows.astype(BF)

    def w_first():
        for m in range(2):
            w_go(s, m, xnb)
        w_go(s, 0, zup)
        w_go(s, 1, zup)
        for m in range(2):
            w_go(s, m, sib)

    def w_second():
        w_go(s, 1, zdn)
        w_go(s, 0, zdn)

    def comm_of(entries):
        plan = []
        for part, (cond, slot, forward, relays) in entries:
            sends = relays + [(cond if forward is None else cond & forward, sib)] * (forward is not False)
            numbered = []
            for ok, dev in sends:
                numbered.append((ok, dev, len(kv_sent)))
                kv_sent.append((ok, slot, part, dev))
            plan.append((cond, slot, part, numbered))

        def run():
            for cond, slot, part, numbered in plan:

                @pl.when(cond)
                def _(slot=slot, part=part):
                    kv_arrived(slot, part)

                for ok, dev, sem in numbered:

                    @pl.when(ok)
                    def _(slot=slot, part=part, dev=dev, sem=sem):
                        kv_send(slot, part, dev, sem).start()

        return run

    middle = (z == 1) | (z == 2)
    up1 = (up_ok(-1), up_slot(-1, c), None, [(middle, zup)])
    over = (down_ok(0), down_slot(0, c), c == 1, [((x == 1) & (z >= 1), zdn), ((x == 1) & (z == 3), zup)])
    down1 = (down_ok(1), down_slot(1, c), None, [((x == 1) & middle, zdn)])
    down1v = (down_ok(1), down_slot(1, c), None, [])
    side1 = ((x == 0) & middle, down_slot(1, c), False, [((x == 0) & middle, zdn)])
    side2 = ((x == 0) & (z <= 1), down_slot(2, c), False, [((x == 0) & (z <= 1), xnb)])
    up3 = (up_ok(-3), up_slot(-3, c), None, [])
    down3 = (down_ok(3), down_slot(3, c), None, [])
    up2 = (up_ok(-2), up_slot(-2, c), None, [])
    down2 = (down_ok(2), down_slot(2, c), None, [])
    comm_a = comm_of([(0, over), (0, up1), (1, side1), (1, over), (1, up1)])
    comm_b0 = comm_of([(0, down1), (1, side2)])
    comm_b1 = comm_of([(1, down1v), (0, up3), (1, up3), (0, down3), (1, down3)])
    comm_c = comm_of([(0, up2), (0, down2), (1, up2), (1, down2)])

    offsets = {2: -1, 3: 0, 4: -1, 5: 0, 6: 1, 7: -3, 8: 3, 9: 1, 10: -3, 11: 3, 12: -2, 13: 2, 14: -2, 15: 2}

    def step(i, carry):
        @pl.when(i == 2)
        def _():
            comm_a()

        @pl.when(i == 4)
        def _():
            comm_b0()
            repack()
            w_first()

        @pl.when(i == 6)
        def _():
            comm_b1()
            w_second()

        @pl.when(i == 12)
        def _():
            comm_c()

        off = 0
        for k, value in offsets.items():
            off = off + jnp.where(i == k, value, 0)
        from_sib = (i == 1) | (i == 4) | (i == 5) | ((i >= 9) & (i <= 11)) | (i >= 14)
        is_down = (i >= 2) & (off >= 0)
        column = jnp.where(is_down, 0, x)
        zz = z + off
        ok = jnp.where(is_down, (x == 1) & (zz <= 3), zz >= 0)
        ok = ok & ((i != 1) | (c == 1)) & ((i != 5) | (c == 0))
        core = jnp.where(from_sib, 1 - c, c)
        slot = column * 8 + (zz + 4) % 4 * 2 + core

        @pl.when(ok & from_sib)
        def _():
            kv_arrived(slot, 0)
            kv_arrived(slot, 1)

        @pl.when(ok)
        def _():
            flash(slot, False)

        return carry

    flash(s, True)
    lax.fori_loop(1, 16, step, 0)

    for r in range(2):
        att[:, r * HD : (r + 1) * HD] = (acc[r] / lbuf[r, :, 0:1]).astype(BF)

    s_x = (1 - x) * 8 + z * 2 + c
    s_zm = x * 8 + zm * 2 + c
    s_zp = x * 8 + zp * 2 + c
    s_z2 = x * 8 + (z + 2) % 4 * 2 + c
    s_xzm = (1 - x) * 8 + zm * 2 + c
    s_xzp = (1 - x) * 8 + zp * 2 + c
    s_xz2 = (1 - x) * 8 + (z + 2) % 4 * 2 + c

    def w_share(slot, *halves):
        for m in halves:
            w_arrived(slot, m)
            w_go(slot, m, sib)

    def w_early():
        w_arrived(s_zm, 0)
        w_go(s_zm, 0, zup)
        w_go(s_zm, 0, sib)
        w_arrived(s_zp, 1)
        w_go(s_zp, 1, zdn)

    def w_over():
        w_arrived(s_x, 0)
        w_go(s_x, 0, zup)
        w_arrived(s_x, 1)
        w_go(s_x, 1, zdn)
        w_go(s_x, 1, zup)
        w_go(s_x, 0, zdn)
        w_go(s_x, 0, sib)
        w_go(s_x, 1, sib)
        w_go(s_zp, 1, sib)

    def w_rest():
        w_share(s_zm, 1)
        w_share(s_zp, 0)
        w_share(s_z2, 0)
        w_arrived(s_z2, 1)
        w_go(s_z2, 1, sib)

    def w_late():
        w_arrived(s_xzm, 0)
        w_go(s_xzm, 0, zup)
        w_go(s_xzm, 0, sib)
        w_arrived(s_xzp, 1)
        w_go(s_xzp, 1, zdn)
        w_go(s_xzp, 1, sib)

    def w_last():
        w_share(s_xzp, 0)
        w_share(s_xzm, 1)

    def w_end():
        w_share(s_xz2, 0, 1)
        for xx in range(2):
            for zz in range(4):
                for m in range(2):
                    w_arrived(xx * 8 + zz * 2 + 1 - c, m)

    rs_sent = []

    def send(src, dst, recv, dev):
        copy = rcopy(src, dst, rs_s.at[len(rs_sent)], recv, dev)
        copy.start()
        rs_sent.append(copy)

    def rows_of(block):
        return pl.ds(al(block * BLK, 16), BLK)

    cols = (
        (pl.ds(0, PART_A // 2), pl.ds(PART_A // 2, PART_A // 2)),
        (pl.ds(PART_A, PART_B // 2), pl.ds(PART_A + PART_B // 2, PART_B // 2)),
    )
    first = pl.ds(0, PART_A)
    lanes = ((1, o), (1, h), (0, h))

    def r1_at(k, lane, way):
        return r1b.at[k, lane, way] if lane < 2 else r1a.at[k, way]

    def r2_at(k, lane, way, half):
        return r2b.at[k, lane, way, half] if lane < 2 else r2a.at[k, way, half]

    def arrived(ref, recv):
        rcopy(ref, ref, rs_s.at[0], recv, xhi).wait_recv()

    def rs_far(k, pb, lane):
        part, g = lanes[lane]
        far = rows_of(g * 4 + y2)
        send(pb.at[far, cols[part][0]], r1_at(k, lane, 0), r1_r.at[k, lane, 0], yup)
        send(pb.at[far, cols[part][1]], r1_at(k, lane, 1), r1_r.at[k, lane, 1], ydn)

    def rs_near(k, pb, lane):
        part, g = lanes[lane]
        send(pb.at[rows_of(g * 4 + yp), cols[part][1]], r2_at(k, lane, 0, 1), r2_r.at[k, lane, 0, 1], yup)
        send(pb.at[rows_of(g * 4 + ym), cols[part][0]], r2_at(k, lane, 1, 0), r2_r.at[k, lane, 1, 0], ydn)

    def rs_middle(k, pb, lane):
        part, g = lanes[lane]
        for way, (yy, dev) in enumerate(((yp, yup), (ym, ydn))):
            near = rows_of(g * 4 + yy)
            ref = r1_at(k, lane, way)
            arrived(ref, r1_r.at[k, lane, way])
            pb[near, cols[part][way]] = (
                pb[near, cols[part][way]].astype(F32) + ref[...].astype(F32)
            ).astype(BF)
            send(pb.at[near, cols[part][way]], r2_at(k, lane, way, way), r2_r.at[k, lane, way, way], dev)

    def rs_end(k, pb, lane):
        part, g = lanes[lane]
        for way in range(2):
            for half in range(2):
                arrived(r2_at(k, lane, way, half), r2_r.at[k, lane, way, half])
        mine = rows_of(g * 4 + y)
        return jnp.concatenate(
            [
                pb[mine, cols[part][half]].astype(F32)
                + r2_at(k, lane, 0, half)[...].astype(F32)
                + r2_at(k, lane, 1, half)[...].astype(F32)
                for half in range(2)
            ],
            axis=1,
        )

    def rs_over(k, pb):
        for yy in (y2, yp, ym, y):
            send(pb.at[rows_of(o * 4 + yy), first], rxa.at[k, yy], rxa_r.at[k, yy], xhi)

    def rs_add(k, pb, yy):
        arrived(rxa.at[k, yy], rxa_r.at[k, yy])
        at = rows_of(h * 4 + yy)
        pb[at, first] = (pb[at, first].astype(F32) + rxa[k, yy].astype(F32)).astype(BF)

    def tp_sum(k, lhs, weight, pb, pump0, pump2, pump1):
        project(lhs, weight, o, pb)
        rs_over(k, pb)
        rs_far(k, pb, 0)
        rs_near(k, pb, 0)
        project(lhs, weight, h, pb)
        rs_middle(k, pb, 0)
        pump0()
        rs_add(k, pb, y2)
        rs_far(k, pb, 2)
        rs_far(k, pb, 1)
        rs_near(k, pb, 1)
        sx[k] = rs_end(k, pb, 0).astype(BF)
        send(sx.at[k], rx.at[k], rx_r.at[k], xhi)
        pump2()
        rs_middle(k, pb, 1)
        rs_add(k, pb, yp)
        rs_add(k, pb, ym)
        rs_near(k, pb, 2)
        rs_middle(k, pb, 2)
        pump1()
        part_b = rs_end(k, pb, 1)
        arrived(rxa.at[k, y], rxa_r.at[k, y])
        part_a = rs_end(k, pb, 2) + rxa[k, y].astype(F32)
        arrived(rx.at[k], rx_r.at[k])
        return jnp.concatenate([part_a, part_b + rx[k].astype(F32)], axis=1)

    def normed(values, gain):
        meansq = jnp.mean(values * values, axis=-1, keepdims=True)
        return values * lax.rsqrt(meansq + 1e-06) * gain[...].reshape(1, D)

    ag_sent = []

    def ag_copy(k, ag, block, part, half, dev, sem):
        ref = ag.at[rows_of(block), cols[part][half]]
        return rcopy(ref, ref, ag_s.at[sem], ag_r.at[k, block, part * 2 + half], dev)

    def ag_go(k, ag, block, part, half, dev):
        copy = ag_copy(k, ag, block, part, half, dev, len(ag_sent))
        copy.start()
        ag_sent.append(copy)

    def ag_arrived(k, ag, block, part, half):
        ag_copy(k, ag, block, part, half, xhi, 0).wait_recv()

    def ag_both(k, ag, block, part):
        ag_go(k, ag, block, part, 0, yup)
        ag_go(k, ag, block, part, 1, ydn)
        ag_go(k, ag, block, part, 1, yup)
        ag_go(k, ag, block, part, 0, ydn)

    def ag_relay(k, ag, g, part):
        ag_arrived(k, ag, g * 4 + ym, part, 0)
        ag_go(k, ag, g * 4 + ym, part, 0, yup)
        ag_arrived(k, ag, g * 4 + yp, part, 1)
        ag_go(k, ag, g * 4 + yp, part, 1, ydn)

    def ag_rest(k, ag, g, part):
        ag_arrived(k, ag, g * 4 + ym, part, 1)
        ag_arrived(k, ag, g * 4 + yp, part, 0)

    def ag_far(k, ag, g, part):
        ag_arrived(k, ag, g * 4 + y2, part, 0)
        ag_arrived(k, ag, g * 4 + y2, part, 1)

    def tp_gather(k, ag, pump0, pump1):
        own = h * 4 + y
        for half in range(2):
            ag_go(k, ag, own, 1, half, xhi)
        ag_both(k, ag, own, 0)
        for half in range(2):
            ag_go(k, ag, own, 0, half, xhi)
        ag_both(k, ag, own, 1)
        ag_relay(k, ag, h, 0)
        ag_rest(k, ag, h, 0)
        for yy in (ym, yp):
            for half in range(2):
                ag_go(k, ag, h * 4 + yy, 0, half, xhi)
        pump0()
        for half in range(2):
            ag_arrived(k, ag, o * 4 + y, 1, half)
        ag_relay(k, ag, h, 1)
        ag_both(k, ag, o * 4 + y, 1)
        ag_far(k, ag, h, 0)
        for half in range(2):
            ag_go(k, ag, h * 4 + y2, 0, half, xhi)
        pump1()
        ag_relay(k, ag, o, 1)
        ag_rest(k, ag, h, 1)
        ag_far(k, ag, h, 1)

    def tp_gathered(k, ag):
        ag_rest(k, ag, o, 1)
        ag_far(k, ag, o, 1)
        for yy in range(4):
            for half in range(2):
                ag_arrived(k, ag, o * 4 + yy, 0, half)

    def group_rows(g):
        return pl.ds(al(g * GROUP, 16), GROUP)

    def project(lhs, weight, g, pb):
        def tile(j, carry):
            at = pl.ds(al(j * 256, 256), 256)
            pb[group_rows(g), at] = jnp.dot(
                lhs[group_rows(g), :], weight[:, at], preferred_element_type=F32
            ).astype(BF)
            return carry

        lax.fori_loop(0, D // 256, tile, 0)

    def nothing():
        pass

    local_copies[4].wait()
    total = tp_sum(0, att, owv, pb1, w_early, w_over, w_rest)
    local_copies[5].wait()
    mid = hidv[...].astype(F32) + normed(total, g_attn)
    resid[...] = mid
    ag1[rows_of(own_block), :] = normed(mid, g_pre).astype(BF)
    tp_gather(0, ag1, w_late, w_last)
    w_end()

    def ffn(g):
        def tile(j, carry):
            at = pl.ds(al(j * 128, 128), 128)
            both = jnp.concatenate([wbuf[0, :, at], wbuf[1, :, at]], axis=1)
            joint = jnp.dot(ag1[group_rows(g), :], both, preferred_element_type=F32)
            gate = joint[:, :128]
            up = joint[:, 128:]
            inner = 0.7978845608028654 * (gate + 0.044715 * (gate * gate * gate))
            act[group_rows(g), at] = (0.5 * gate * (1.0 + jnp.tanh(inner)) * up).astype(BF)
            return carry

        lax.fori_loop(0, UNITS // 128, tile, 0)

    ffn(h)
    tp_gathered(0, ag1)
    ffn(o)
    local_copies[6].wait()
    total = tp_sum(1, act, dwv, pb2, nothing, nothing, nothing)
    last = resid[...] + normed(total, g_post)
    ag2[rows_of(own_block), :] = normed(last, g_next).astype(BF)
    tp_gather(1, ag2, nothing, nothing)
    local_copies[7].wait()

    def next_qkv(g):
        def tile(j, carry):
            at = pl.ds(al(j * 256, 256), 256)
            out[group_rows(g), at] = jnp.dot(
                ag2[group_rows(g), :], nwv[:, at], preferred_element_type=F32
            ).astype(BF)
            return carry

        lax.fori_loop(0, QKV // 256, tile, 0)

    next_qkv(h)
    tp_gathered(1, ag2)
    next_qkv(o)

    for sem, (cond, slot, part, dev) in enumerate(kv_sent):

        @pl.when(cond)
        def _(slot=slot, part=part, dev=dev, sem=sem):
            kv_send(slot, part, dev, sem).wait_send()

    for k in range(1, 8):
        a_send(k).wait_send()
    for sem, (slot, m, dev) in enumerate(w_sent):
        w_copy(slot, m, dev, sem).wait_send()
    for copy in rs_sent + ag_sent:
        copy.wait_send()


def local(hid, joined, lengths, ow, gu, dw, nw, g_attn, g_pre, g_post, g_next):
    hbm = pl.BlockSpec(memory_space=pl.ANY)
    vmem = pl.BlockSpec(memory_space=pltpu.VMEM)
    smem = pl.BlockSpec(memory_space=pltpu.SMEM)
    V = pltpu.VMEM
    DMA = pltpu.SemaphoreType.DMA
    scratch = [
        V((2, ROWS, HD), BF),
        V((16, 2, ROWS, HD), BF),
        V(ow.shape, BF),
        V(dw.shape, BF),
        V(nw.shape, BF),
        V((BLK, D), BF),
        V((2, PIECE, gu.shape[2]), F32),
        V((8, 2, PIECE, UNITS), BF),
        V((8, 2, PIECE, UNITS), BF),
        V((2, D, UNITS), BF),
        V((ROWS, 1), jnp.int32),
        V((2, ROWS, 1), F32),
        V((2, ROWS, 1), F32),
        V((2, ROWS, HD), F32),
        V((ROWS, 2 * HD), BF),
        V((ROWS, D), BF),
        V((ROWS, D), BF),
        V((2, 2, 2, BLK, PART_B // 2), BF),
        V((2, 2, 2, 2, BLK, PART_B // 2), BF),
        V((2, 2, BLK, PART_A // 2), BF),
        V((2, 2, 2, BLK, PART_A // 2), BF),
        V((2, 4, BLK, PART_A), BF),
        V((2, BLK, PART_B), BF),
        V((2, BLK, PART_B), BF),
        V((ROWS, D), BF),
        V((ROWS, D), BF),
        V((ROWS, UNITS), BF),
        V((BLK, D), F32),
        DMA((10,)),
        DMA((36,)),
        DMA((16, 2)),
        DMA((8,)),
        DMA((8,)),
        DMA((48,)),
        DMA((16, 2)),
        DMA((2, 3, 2)),
        DMA((2, 3, 2, 2)),
        DMA((2, 4)),
        DMA((2,)),
        DMA((48,)),
        DMA((64,)),
        DMA((2, 8, 4)),
    ]
    return pl.pallas_call(
        kernel,
        out_shape=jax.ShapeDtypeStruct((ROWS, QKV), BF),
        in_specs=[smem, hbm, hbm, hbm, hbm, hbm, hbm, vmem, vmem, vmem, vmem],
        out_specs=vmem,
        scratch_shapes=scratch,
        compiler_params=pltpu.CompilerParams(
            collective_id=0, has_side_effects=True, vmem_limit_bytes=67043328
        ),
    )(
        lengths, hid, joined, ow, gu.transpose(1, 0, 2), dw, nw,
        g_attn, g_pre, g_post, g_next,
    )


def solution(mesh):
    in_specs = (
        P("seq", None),
        P("seq", "tp"),
        P(),
        P("tp", None),
        P(None, ("seq", "tp"), None),
        P("tp", None),
        P(None, "tp"),
        P(),
        P(),
        P(),
        P(),
    )
    return jax.shard_map(
        local, mesh=mesh, in_specs=in_specs, out_specs=P("seq", "tp"), check_vma=False
    )
```

```python
import jax
import jax.numpy as jnp
from jax import lax
from jax.experimental import pallas as pl
from jax.experimental.pallas import tpu as pltpu
from jax.sharding import PartitionSpec as P

MESH = pl.DeviceIdType.MESH
BF = jnp.bfloat16
F32 = jnp.float32
D = 3584
PART_A = 1536
PART_B = D - PART_A
ROWS = 384
HD = 256
UNITS = 896
PIECE = 28
CHUNK = 224
BLK = 48
GROUP = 192
QKV = 1024
NEG = -1e30


def al(value, to):
    return pl.multiple_of(value, to)


def kernel(
    lens, hid, joined, ow, gu, dw, nw, g_attn, g_pre, g_post, g_next,
    out,
    qbuf, kvbuf, owv, dwv, nwv, hidv, guv, gub, abuf, wbuf,
    lowbuf, mbuf, lbuf, acc, att, pb1, pb2, r1b, r2b, r1a, r2a, rxa, rx, sx, ag1, ag2, act, resid,
    lsem, kv_s, kv_r, a_s, a_r, w_s, w_r, r1_r, r2_r, rxa_r, rx_r, rs_s, ag_s, ag_r,
):
    s = lax.axis_index("seq")
    t = lax.axis_index("tp")
    x = s // 8
    z = (s // 2) % 4
    c = s % 2
    y = t // 2
    h = t % 2
    o = 1 - h

    def dev_seq(xx, zz, cc):
        return (xx * 8 + zz * 2 + cc, t)

    def dev_tp(yy, hh):
        return (s, yy * 2 + hh)

    zp, zm = (z + 1) % 4, (z + 3) % 4
    yp, ym, y2 = (y + 1) % 4, (y + 3) % 4, (y + 2) % 4
    sib = dev_seq(x, z, 1 - c)
    xnb = dev_seq(1 - x, z, c)
    zup = dev_seq(x, zp, c)
    zdn = dev_seq(x, zm, c)
    yup = dev_tp(yp, h)
    ydn = dev_tp(ym, h)
    xhi = dev_tp(y, o)

    barrier = pltpu.get_barrier_semaphore()
    tp_peers = [(s, (t + k) % 8) for k in range(1, 8)]
    for peer in [sib, xnb, zup, zdn] + tp_peers:
        pl.semaphore_signal(barrier, inc=1, device_id=peer, device_id_type=MESH)

    own_block = h * 4 + y
    loads = [
        (joined.at[:, pl.ds(512, 256)], kvbuf.at[s, 0]),
        (joined.at[:, pl.ds(0, 256)], qbuf.at[0]),
        (joined.at[:, pl.ds(256, 256)], qbuf.at[1]),
        (gu.at[:, 0, :], guv.at[0]),
        (ow, owv),
        (hid.at[pl.ds(al(own_block * BLK, 16), BLK), :], hidv),
        (dw, dwv),
        (nw, nwv),
        (joined.at[:, pl.ds(768, 256)], kvbuf.at[s, 1]),
        (gu.at[:, 1, :], guv.at[1]),
    ]
    local_copies = [
        pltpu.make_async_copy(src, dst, lsem.at[i]) for i, (src, dst) in enumerate(loads)
    ]
    for i in (0, 8, 9, 3, 1, 2):
        local_copies[i].start()

    def rcopy(src, dst, send, recv, dev):
        return pltpu.make_async_remote_copy(
            src_ref=src,
            dst_ref=dst,
            send_sem=send,
            recv_sem=recv,
            device_id=dev,
            device_id_type=MESH,
        )

    pl.semaphore_wait(barrier, 11)

    def kv_send(slot, part, dev, sem):
        ref = kvbuf.at[slot, part]
        return rcopy(ref, ref, kv_s.at[sem], kv_r.at[slot, part], dev)

    def kv_arrived(slot, part):
        kv_send(slot, part, sib, 0).wait_recv()

    kv_sent = []
    for part in range(2):
        local_copies[(0, 8)[part]].wait()
        outs = [(z < 3, zup), (x == 0, xnb), (z == 0, zdn), (c == 0, sib)]
        if part == 1:
            outs.append(((x == 0) & (z >= 2), zdn))
        for ok, dev in outs:
            sem = len(kv_sent)
            kv_sent.append((ok, s, part, dev))

            @pl.when(ok)
            def _(part=part, dev=dev, sem=sem):
                kv_send(s, part, dev, sem).start()

    def a_send(k, m):
        peer = (t + k) % 8
        return rcopy(gub.at[peer, m], abuf.at[t, m], a_s.at[k, m], a_r.at[k, m], (s, peer))

    for m in (1, 0):
        local_copies[(3, 9)[m]].wait()
        for k in range(8):
            gub[k, m] = guv[m, :, k * UNITS : (k + 1) * UNITS].astype(BF)
        for k in range(1, 8):
            a_send(k, m).start()
    for i in (4, 5, 6, 7):
        local_copies[i].start()

    local_copies[1].wait()
    local_copies[2].wait()
    end0 = lens[0]
    end1 = end0 + lens[1]
    end2 = end1 + lens[2]

    place = s * ROWS + lax.broadcasted_iota(jnp.int32, (ROWS, 1), 0)
    low = jnp.where(
        place >= end2,
        end2,
        jnp.where(place >= end1, end1, jnp.where(place >= end0, end0, 0)),
    )
    lowbuf[...] = low

    def flash(slot, own):
        other = slot * ROWS + lax.broadcasted_iota(jnp.int32, (ROWS, ROWS), 1)
        allowed = other >= lowbuf[...]
        if own:
            allowed = allowed & (other <= place)
        for r in range(2):
            scores = lax.dot_general(
                qbuf[r],
                kvbuf[slot, 0],
                (((1,), (1,)), ((), ())),
                preferred_element_type=F32,
            ) * (HD ** -0.5 * 1.4426950408889634)
            scores = jnp.where(allowed, scores, NEG)
            peak = jnp.max(scores, axis=-1, keepdims=True)
            if not own:
                before = mbuf[r]
                peak = jnp.maximum(before, peak)
            weights = jnp.exp2(scores - peak)
            total = jnp.sum(weights, axis=-1, keepdims=True)
            blend = jnp.dot(weights.astype(BF), kvbuf[slot, 1], preferred_element_type=F32)
            if not own:
                fade = jnp.exp2(before - peak)
                total = total + lbuf[r] * fade
                blend = blend + acc[r] * fade
            lbuf[r] = total
            mbuf[r] = peak
            acc[r] = blend

    def up_ok(off):
        return z + off >= 0

    def down_ok(off):
        return (x == 1) & (z + off <= 3)

    def up_slot(off, core):
        return x * 8 + (z + off + 4) % 4 * 2 + core

    def down_slot(off, core):
        return (z + off) % 4 * 2 + core

    def w_ref(slot, m):
        return wbuf.at[m, pl.ds(al(slot * CHUNK, 16), CHUNK), :]

    w_sent = []

    def w_copy(slot, m, dev, sem):
        return rcopy(w_ref(slot, m), w_ref(slot, m), w_s.at[sem], w_r.at[slot, m], dev)

    def w_go(slot, m, dev):
        w_copy(slot, m, dev, len(w_sent)).start()
        w_sent.append((slot, m, dev))

    def w_arrived(slot, m):
        w_copy(slot, m, sib, 0).wait_recv()

    def repack(m):
        for k in range(1, 8):
            peer = (t + 8 - k) % 8
            rcopy(gub.at[0, m], abuf.at[peer, m], a_s.at[k, m], a_r.at[k, m], (s, peer)).wait_recv()
        abuf[t, m] = gub[t, m]
        rows = jnp.concatenate([abuf[k, m].astype(F32) for k in range(8)], axis=0)
        wbuf[m, pl.ds(al(s * CHUNK, 16), CHUNK), :] = rows.astype(BF)

    def w_first():
        repack(1)
        w_go(s, 1, zdn)
        w_go(s, 1, xnb)
        repack(0)
        w_go(s, 0, zup)
        w_go(s, 0, zdn)
        w_go(s, 0, xnb)
        w_go(s, 1, zup)
        for m in range(2):
            w_go(s, m, sib)

    def comm_of(entries):
        plan = []
        for part, (cond, slot, forward, relays) in entries:
            sends = relays + [(cond if forward is None else cond & forward, sib)] * (forward is not False)
            numbered = []
            for ok, dev in sends:
                numbered.append((ok, dev, len(kv_sent)))
                kv_sent.append((ok, slot, part, dev))
            plan.append((cond, slot, part, numbered))

        def run():
            for cond, slot, part, numbered in plan:

                @pl.when(cond)
                def _(slot=slot, part=part):
                    kv_arrived(slot, part)

                for ok, dev, sem in numbered:

                    @pl.when(ok)
                    def _(slot=slot, part=part, dev=dev, sem=sem):
                        kv_send(slot, part, dev, sem).start()

        return run

    middle = (z == 1) | (z == 2)
    up1 = (up_ok(-1), up_slot(-1, c), None, [(middle, zup)])
    over = (down_ok(0), down_slot(0, c), c == 1, [((x == 1) & (z >= 1), zdn), ((x == 1) & (z == 3), zup)])
    down1 = (down_ok(1), down_slot(1, c), None, [((x == 1) & middle, zdn)])
    down1v = (down_ok(1), down_slot(1, c), None, [])
    side1 = ((x == 0) & middle, down_slot(1, c), False, [((x == 0) & middle, zdn)])
    side2 = ((x == 0) & (z <= 1), down_slot(2, c), False, [((x == 0) & (z <= 1), xnb)])
    up3 = (up_ok(-3), up_slot(-3, c), None, [])
    down3 = (down_ok(3), down_slot(3, c), None, [])
    up2 = (up_ok(-2), up_slot(-2, c), None, [])
    down2 = (down_ok(2), down_slot(2, c), None, [])
    comm_a = comm_of([(0, over), (0, up1), (1, side1), (1, over), (1, up1)])
    comm_b0 = comm_of([(0, down1), (1, side2)])
    comm_b1 = comm_of([(1, down1v), (0, up3), (1, up3), (0, down3), (1, down3)])
    comm_c = comm_of([(0, up2), (0, down2), (1, up2), (1, down2)])

    offsets = {2: -1, 3: 0, 4: -1, 5: 0, 6: 1, 7: -3, 8: 3, 9: 1, 10: -3, 11: 3, 12: -2, 13: 2, 14: -2, 15: 2}

    def step(i, carry):
        @pl.when(i == 2)
        def _():
            comm_a()

        @pl.when(i == 4)
        def _():
            comm_b0()
            w_first()

        @pl.when(i == 6)
        def _():
            comm_b1()

        @pl.when(i == 12)
        def _():
            comm_c()

        off = 0
        for k, value in offsets.items():
            off = off + jnp.where(i == k, value, 0)
        from_sib = (i == 1) | (i == 4) | (i == 5) | ((i >= 9) & (i <= 11)) | (i >= 14)
        is_down = (i >= 2) & (off >= 0)
        column = jnp.where(is_down, 0, x)
        zz = z + off
        ok = jnp.where(is_down, (x == 1) & (zz <= 3), zz >= 0)
        ok = ok & ((i != 1) | (c == 1)) & ((i != 5) | (c == 0))
        core = jnp.where(from_sib, 1 - c, c)
        slot = column * 8 + (zz + 4) % 4 * 2 + core

        @pl.when(ok & from_sib)
        def _():
            kv_arrived(slot, 0)
            kv_arrived(slot, 1)

        @pl.when(ok)
        def _():
            flash(slot, False)

        return carry

    flash(s, True)
    lax.fori_loop(1, 16, step, 0)

    for r in range(2):
        att[:, r * HD : (r + 1) * HD] = (acc[r] / lbuf[r, :, 0:1]).astype(BF)

    s_x = (1 - x) * 8 + z * 2 + c
    s_zm = x * 8 + zm * 2 + c
    s_zp = x * 8 + zp * 2 + c
    s_z2 = x * 8 + (z + 2) % 4 * 2 + c
    s_xzm = (1 - x) * 8 + zm * 2 + c
    s_xzp = (1 - x) * 8 + zp * 2 + c
    s_xz2 = (1 - x) * 8 + (z + 2) % 4 * 2 + c

    def w_share(slot, *halves):
        for m in halves:
            w_arrived(slot, m)
            w_go(slot, m, sib)

    def w_early():
        w_arrived(s_zm, 0)
        w_go(s_zm, 0, zup)
        w_go(s_zm, 0, sib)
        w_arrived(s_zp, 1)
        w_go(s_zp, 1, zdn)

    def w_over():
        w_arrived(s_x, 1)
        w_go(s_x, 1, zdn)
        w_arrived(s_x, 0)
        w_go(s_x, 0, zup)
        w_go(s_x, 1, zup)
        w_go(s_x, 0, zdn)
        w_go(s_x, 0, sib)
        w_go(s_x, 1, sib)
        w_go(s_zp, 1, sib)

    def w_rest():
        w_share(s_zm, 1)
        w_share(s_zp, 0)
        w_share(s_z2, 0)
        w_arrived(s_z2, 1)
        w_go(s_z2, 1, sib)

    def w_late():
        w_arrived(s_xzm, 0)
        w_go(s_xzm, 0, zup)
        w_go(s_xzm, 0, sib)
        w_arrived(s_xzp, 1)
        w_go(s_xzp, 1, zdn)
        w_go(s_xzp, 1, sib)

    def w_last():
        w_share(s_xzp, 0)
        w_share(s_xzm, 1)

    def w_end():
        w_share(s_xz2, 0, 1)
        for xx in range(2):
            for zz in range(4):
                for m in range(2):
                    w_arrived(xx * 8 + zz * 2 + 1 - c, m)

    rs_sent = []

    def send(src, dst, recv, dev):
        copy = rcopy(src, dst, rs_s.at[len(rs_sent)], recv, dev)
        copy.start()
        rs_sent.append(copy)

    def rows_of(block):
        return pl.ds(al(block * BLK, 16), BLK)

    cols = (
        (pl.ds(0, PART_A // 2), pl.ds(PART_A // 2, PART_A // 2)),
        (pl.ds(PART_A, PART_B // 2), pl.ds(PART_A + PART_B // 2, PART_B // 2)),
    )
    first = pl.ds(0, PART_A)
    lanes = ((1, o), (1, h), (0, h))

    def r1_at(k, lane, way):
        return r1b.at[k, lane, way] if lane < 2 else r1a.at[k, way]

    def r2_at(k, lane, way, half):
        return r2b.at[k, lane, way, half] if lane < 2 else r2a.at[k, way, half]

    def arrived(ref, recv):
        rcopy(ref, ref, rs_s.at[0], recv, xhi).wait_recv()

    def rs_far(k, pb, lane):
        part, g = lanes[lane]
        far = rows_of(g * 4 + y2)
        send(pb.at[far, cols[part][0]], r1_at(k, lane, 0), r1_r.at[k, lane, 0], yup)
        send(pb.at[far, cols[part][1]], r1_at(k, lane, 1), r1_r.at[k, lane, 1], ydn)

    def rs_near(k, pb, lane):
        part, g = lanes[lane]
        send(pb.at[rows_of(g * 4 + yp), cols[part][1]], r2_at(k, lane, 0, 1), r2_r.at[k, lane, 0, 1], yup)
        send(pb.at[rows_of(g * 4 + ym), cols[part][0]], r2_at(k, lane, 1, 0), r2_r.at[k, lane, 1, 0], ydn)

    def rs_middle(k, pb, lane):
        part, g = lanes[lane]
        for way, (yy, dev) in enumerate(((yp, yup), (ym, ydn))):
            near = rows_of(g * 4 + yy)
            ref = r1_at(k, lane, way)
            arrived(ref, r1_r.at[k, lane, way])
            pb[near, cols[part][way]] = (
                pb[near, cols[part][way]].astype(F32) + ref[...].astype(F32)
            ).astype(BF)
            send(pb.at[near, cols[part][way]], r2_at(k, lane, way, way), r2_r.at[k, lane, way, way], dev)

    def rs_end(k, pb, lane):
        part, g = lanes[lane]
        for way in range(2):
            for half in range(2):
                arrived(r2_at(k, lane, way, half), r2_r.at[k, lane, way, half])
        mine = rows_of(g * 4 + y)
        return jnp.concatenate(
            [
                pb[mine, cols[part][half]].astype(F32)
                + r2_at(k, lane, 0, half)[...].astype(F32)
                + r2_at(k, lane, 1, half)[...].astype(F32)
                for half in range(2)
            ],
            axis=1,
        )

    def rs_over(k, pb):
        for yy in (y2, yp, ym, y):
            send(pb.at[rows_of(o * 4 + yy), first], rxa.at[k, yy], rxa_r.at[k, yy], xhi)

    def rs_add(k, pb, yy):
        arrived(rxa.at[k, yy], rxa_r.at[k, yy])
        at = rows_of(h * 4 + yy)
        pb[at, first] = (pb[at, first].astype(F32) + rxa[k, yy].astype(F32)).astype(BF)

    def tp_sum(k, lhs, weight, pb, pump0, pump2, pump1):
        project(lhs, weight, o, pb)
        rs_over(k, pb)
        rs_far(k, pb, 0)
        rs_near(k, pb, 0)
        project(lhs, weight, h, pb)
        rs_middle(k, pb, 0)
        pump0()
        rs_add(k, pb, y2)
        rs_far(k, pb, 2)
        rs_far(k, pb, 1)
        rs_near(k, pb, 1)
        sx[k] = rs_end(k, pb, 0).astype(BF)
        send(sx.at[k], rx.at[k], rx_r.at[k], xhi)
        pump2()
        rs_middle(k, pb, 1)
        rs_add(k, pb, yp)
        rs_add(k, pb, ym)
        rs_near(k, pb, 2)
        rs_middle(k, pb, 2)
        pump1()
        part_b = rs_end(k, pb, 1)
        arrived(rxa.at[k, y], rxa_r.at[k, y])
        part_a = rs_end(k, pb, 2) + rxa[k, y].astype(F32)
        arrived(rx.at[k], rx_r.at[k])
        return jnp.concatenate([part_a, part_b + rx[k].astype(F32)], axis=1)

    def normed(values, gain):
        meansq = jnp.mean(values * values, axis=-1, keepdims=True)
        return values * lax.rsqrt(meansq + 1e-06) * gain[...].reshape(1, D)

    ag_sent = []

    def ag_copy(k, ag, block, part, half, dev, sem):
        ref = ag.at[rows_of(block), cols[part][half]]
        return rcopy(ref, ref, ag_s.at[sem], ag_r.at[k, block, part * 2 + half], dev)

    def ag_go(k, ag, block, part, half, dev):
        copy = ag_copy(k, ag, block, part, half, dev, len(ag_sent))
        copy.start()
        ag_sent.append(copy)

    def ag_arrived(k, ag, block, part, half):
        ag_copy(k, ag, block, part, half, xhi, 0).wait_recv()

    def ag_both(k, ag, block, part):
        ag_go(k, ag, block, part, 0, yup)
        ag_go(k, ag, block, part, 1, ydn)
        ag_go(k, ag, block, part, 1, yup)
        ag_go(k, ag, block, part, 0, ydn)

    def ag_relay(k, ag, g, part):
        ag_arrived(k, ag, g * 4 + ym, part, 0)
        ag_go(k, ag, g * 4 + ym, part, 0, yup)
        ag_arrived(k, ag, g * 4 + yp, part, 1)
        ag_go(k, ag, g * 4 + yp, part, 1, ydn)

    def ag_rest(k, ag, g, part):
        ag_arrived(k, ag, g * 4 + ym, part, 1)
        ag_arrived(k, ag, g * 4 + yp, part, 0)

    def ag_far(k, ag, g, part):
        ag_arrived(k, ag, g * 4 + y2, part, 0)
        ag_arrived(k, ag, g * 4 + y2, part, 1)

    def tp_gather(k, ag, pump0, pump1):
        own = h * 4 + y
        for half in range(2):
            ag_go(k, ag, own, 1, half, xhi)
        ag_both(k, ag, own, 0)
        for half in range(2):
            ag_go(k, ag, own, 0, half, xhi)
        ag_both(k, ag, own, 1)
        ag_relay(k, ag, h, 0)
        ag_rest(k, ag, h, 0)
        for yy in (ym, yp):
            for half in range(2):
                ag_go(k, ag, h * 4 + yy, 0, half, xhi)
        pump0()
        for half in range(2):
            ag_arrived(k, ag, o * 4 + y, 1, half)
        ag_relay(k, ag, h, 1)
        ag_both(k, ag, o * 4 + y, 1)
        ag_far(k, ag, h, 0)
        for half in range(2):
            ag_go(k, ag, h * 4 + y2, 0, half, xhi)
        pump1()
        ag_relay(k, ag, o, 1)
        ag_rest(k, ag, h, 1)
        ag_far(k, ag, h, 1)

    def tp_gathered(k, ag):
        ag_rest(k, ag, o, 1)
        ag_far(k, ag, o, 1)
        for yy in range(4):
            for half in range(2):
                ag_arrived(k, ag, o * 4 + yy, 0, half)

    def group_rows(g):
        return pl.ds(al(g * GROUP, 16), GROUP)

    def project(lhs, weight, g, pb):
        def tile(j, carry):
            at = pl.ds(al(j * 256, 256), 256)
            pb[group_rows(g), at] = jnp.dot(
                lhs[group_rows(g), :], weight[:, at], preferred_element_type=F32
            ).astype(BF)
            return carry

        lax.fori_loop(0, D // 256, tile, 0)

    def nothing():
        pass

    local_copies[4].wait()
    total = tp_sum(0, att, owv, pb1, w_early, w_over, w_rest)
    local_copies[5].wait()
    mid = hidv[...].astype(F32) + normed(total, g_attn)
    resid[...] = mid
    ag1[rows_of(own_block), :] = normed(mid, g_pre).astype(BF)
    tp_gather(0, ag1, w_late, w_last)
    w_end()

    def ffn(g):
        def tile(j, carry):
            at = pl.ds(al(j * 128, 128), 128)
            both = jnp.concatenate([wbuf[0, :, at], wbuf[1, :, at]], axis=1)
            joint = jnp.dot(ag1[group_rows(g), :], both, preferred_element_type=F32)
            gate = joint[:, :128]
            up = joint[:, 128:]
            inner = 0.7978845608028654 * (gate + 0.044715 * (gate * gate * gate))
            act[group_rows(g), at] = (0.5 * gate * (1.0 + jnp.tanh(inner)) * up).astype(BF)
            return carry

        lax.fori_loop(0, UNITS // 128, tile, 0)

    ffn(h)
    tp_gathered(0, ag1)
    ffn(o)
    local_copies[6].wait()
    total = tp_sum(1, act, dwv, pb2, nothing, nothing, nothing)
    last = resid[...] + normed(total, g_post)
    ag2[rows_of(own_block), :] = normed(last, g_next).astype(BF)
    tp_gather(1, ag2, nothing, nothing)
    local_copies[7].wait()

    def next_qkv(g):
        def tile(j, carry):
            at = pl.ds(al(j * 256, 256), 256)
            out[group_rows(g), at] = jnp.dot(
                ag2[group_rows(g), :], nwv[:, at], preferred_element_type=F32
            ).astype(BF)
            return carry

        lax.fori_loop(0, QKV // 256, tile, 0)

    next_qkv(h)
    tp_gathered(1, ag2)
    next_qkv(o)

    for sem, (cond, slot, part, dev) in enumerate(kv_sent):

        @pl.when(cond)
        def _(slot=slot, part=part, dev=dev, sem=sem):
            kv_send(slot, part, dev, sem).wait_send()

    for k in range(1, 8):
        for m in range(2):
            a_send(k, m).wait_send()
    for sem, (slot, m, dev) in enumerate(w_sent):
        w_copy(slot, m, dev, sem).wait_send()
    for copy in rs_sent + ag_sent:
        copy.wait_send()


def local(hid, joined, lengths, ow, gu, dw, nw, g_attn, g_pre, g_post, g_next):
    hbm = pl.BlockSpec(memory_space=pl.ANY)
    vmem = pl.BlockSpec(memory_space=pltpu.VMEM)
    smem = pl.BlockSpec(memory_space=pltpu.SMEM)
    V = pltpu.VMEM
    DMA = pltpu.SemaphoreType.DMA
    scratch = [
        V((2, ROWS, HD), BF),
        V((16, 2, ROWS, HD), BF),
        V(ow.shape, BF),
        V(dw.shape, BF),
        V(nw.shape, BF),
        V((BLK, D), BF),
        V((2, PIECE, gu.shape[2]), F32),
        V((8, 2, PIECE, UNITS), BF),
        V((8, 2, PIECE, UNITS), BF),
        V((2, D, UNITS), BF),
        V((ROWS, 1), jnp.int32),
        V((2, ROWS, 1), F32),
        V((2, ROWS, 1), F32),
        V((2, ROWS, HD), F32),
        V((ROWS, 2 * HD), BF),
        V((ROWS, D), BF),
        V((ROWS, D), BF),
        V((2, 2, 2, BLK, PART_B // 2), BF),
        V((2, 2, 2, 2, BLK, PART_B // 2), BF),
        V((2, 2, BLK, PART_A // 2), BF),
        V((2, 2, 2, BLK, PART_A // 2), BF),
        V((2, 4, BLK, PART_A), BF),
        V((2, BLK, PART_B), BF),
        V((2, BLK, PART_B), BF),
        V((ROWS, D), BF),
        V((ROWS, D), BF),
        V((ROWS, UNITS), BF),
        V((BLK, D), F32),
        DMA((10,)),
        DMA((36,)),
        DMA((16, 2)),
        DMA((8, 2)),
        DMA((8, 2)),
        DMA((48,)),
        DMA((16, 2)),
        DMA((2, 3, 2)),
        DMA((2, 3, 2, 2)),
        DMA((2, 4)),
        DMA((2,)),
        DMA((48,)),
        DMA((64,)),
        DMA((2, 8, 4)),
    ]
    return pl.pallas_call(
        kernel,
        out_shape=jax.ShapeDtypeStruct((ROWS, QKV), BF),
        in_specs=[smem, hbm, hbm, hbm, hbm, hbm, hbm, vmem, vmem, vmem, vmem],
        out_specs=vmem,
        scratch_shapes=scratch,
        compiler_params=pltpu.CompilerParams(
            collective_id=0, has_side_effects=True, vmem_limit_bytes=67043328
        ),
    )(
        lengths, hid, joined, ow, gu.transpose(1, 0, 2), dw, nw,
        g_attn, g_pre, g_post, g_next,
    )


def solution(mesh):
    in_specs = (
        P("seq", None),
        P("seq", "tp"),
        P(),
        P("tp", None),
        P(None, ("seq", "tp"), None),
        P("tp", None),
        P(None, "tp"),
        P(),
        P(),
        P(),
        P(),
    )
    return jax.shard_map(
        local, mesh=mesh, in_specs=in_specs, out_specs=P("seq", "tp"), check_vma=False
    )
```
